32 devices in a mesh: facet: 8 (over y, x, core), sub: 4 (over z).
Axes of the slice: x: 2, y: 2, z: 4, core: 2. Of those that a mesh axis runs over, the one named last changes fastest.
Arguments:
- facet_spec: bfloat16 [8, 2, 704, 448], P('facet'), may hold values from -3 to 3
- worker_of_subgrid: int32 [32], replicated, may hold values from 0 to 31, each once
- vis_count: int32 [32], P(('facet', 'sub')), may hold values from 512 to 8192, as said below
- bin_offsets: int32 [32, 2, 8192], P(('facet', 'sub')), may hold values from 0 to 248
- bin_fractions: float32 [32, 2, 8192], P(('facet', 'sub')), may hold values from 0 to 1
- observed: float32 [32, 2, 8192], P(('facet', 'sub')), may hold values from -6 to 6
Outputs:
- residual_vis: float32 [32, 2, 8192], P(('facet', 'sub'))
- facet_update: float32 [8, 2, 704, 448], P('facet', None, 'sub')
The draws below stay inside these ranges and needn't reach their ends.
Inputs may be any that keep to these rules, and one draw needn't show every extreme that they name: `worker_of_subgrid`: a permutation of the subgrids. `vis_count`: some device row has all 8192 slots live in every draw.
All inputs are finite; a program needn't handle non-finite values.
Results may differ from the reference program's by a relative error of at most 0.014.
Values may be sent and summed in bfloat16 or wider, within the bound.
A program may use at most 128 MiB of HBM per device.

```python
import math
import jax
import jax.numpy as jnp
from jax import lax

SUB = 256
MC = 256
STEP = 64
KS = 8
VMAX = 8192
POS_V = 4
FACETS = 8
SUBGRIDS = 32
PR = 704
PC = 448


def draw_vis_count(key, part):
    low_key = jax.random.fold_in(key, 11)
    crowd_key = jax.random.fold_in(key, 12)
    pick_key = jax.random.fold_in(key, 13)
    base = jax.random.randint(low_key, (SUBGRIDS,), VMAX // 16, VMAX // 2 + 1)
    crowded = jax.random.randint(crowd_key, (SUBGRIDS,), 0, 8) == 0
    chosen = jax.random.randint(pick_key, (), 0, SUBGRIDS)
    crowded = crowded | (jnp.arange(SUBGRIDS) == chosen)
    return jnp.where(crowded, VMAX, base).astype(jnp.int32)


def set_ends(entries, own_key, least, largest):
    spot = [jax.random.randint(jax.random.fold_in(own_key, axis), (), 0, length) for axis, length in enumerate(entries.shape)]
    main_axis = entries.shape.index(max(entries.shape))
    next_to = spot[:main_axis] + [(spot[main_axis] + 1) % entries.shape[main_axis]] + spot[main_axis + 1:]
    return entries.at[tuple(spot)].set(least).at[tuple(next_to)].set(largest)


def shard_levels(key, dims, split, smallest, largest):
    def one(dim, parts):
        heights = jax.random.uniform(jax.random.fold_in(jax.random.fold_in(key, 6), dim), (parts,), jnp.float32, smallest / len(split), largest / len(split))
        return jnp.repeat(jnp.exp(heights), dims[dim] // parts).reshape((-1,) + (1,) * (len(dims) - dim - 1))

    gain = one(*split[0])
    for cut in split[1:]:
        gain = gain * one(*cut)
    return gain


def scatter_about(key, extent, spread, most, pieces=(), kind=jnp.bfloat16):
    values = spread * jax.random.normal(key, extent, jnp.float32)
    if pieces:
        values = values * shard_levels(key, extent, pieces, -0.22, 0.18)
    return jnp.clip(values, -most, most).astype(kind)


def setup_inputs(seed: int = 0) -> dict:
    arg_keys = jax.random.split(jax.random.key(seed), 7)
    facet_spec = scatter_about(arg_keys[0], (FACETS, 2, PR, PC), 0.5, 3.0, ((0, 8),))
    worker_of_subgrid = jax.random.permutation(arg_keys[1], SUBGRIDS).astype(jnp.int32)
    vis_count = draw_vis_count(jax.random.fold_in(arg_keys[6], 71), 0)
    bin_offsets = set_ends(jax.random.randint(arg_keys[3], (SUBGRIDS, 2, VMAX), 0, SUB - KS + 1), jax.random.fold_in(arg_keys[3], 1), 0, SUB - KS).astype(jnp.int32)
    bin_fractions = jnp.clip(1.0 * jax.random.uniform(arg_keys[4], (SUBGRIDS, 2, VMAX), jnp.float32) ** shard_levels(arg_keys[4], (SUBGRIDS, 2, VMAX), ((0, 32),), -0.2, 0.2), 0.0, 1.0)
    observed = scatter_about(arg_keys[5], (SUBGRIDS, 2, VMAX), 1.0, 6.0, ((0, 32),), jnp.float32)
    return dict(facet_spec=facet_spec, worker_of_subgrid=worker_of_subgrid, vis_count=vis_count, bin_offsets=bin_offsets, bin_fractions=bin_fractions, observed=observed)


TWO_PI = 2.0 * math.pi


def phase_table(offset, facets, swapped, conj_sign):
    sub_index = jnp.arange(SUB, dtype=jnp.int32) - SUB // 2
    win_index = jnp.arange(MC, dtype=jnp.int32) - MC // 2
    if swapped:
        sub_part = sub_index[None, :]
        win_part = win_index[:, None]
    else:
        sub_part = sub_index[:, None]
        win_part = win_index[None, :]
    modulus = SUB * facets
    residue = jnp.mod(sub_part * win_part * facets + sub_part * offset, modulus)
    angles = residue.astype(jnp.float32) * (TWO_PI / modulus)
    factor = MC ** -0.5
    return jnp.stack([jnp.cos(angles) * factor, conj_sign * jnp.sin(angles) * factor]).astype(jnp.bfloat16)


def wide_dot(first_part, second_part):
    return jnp.dot(first_part.astype(jnp.float32), second_part.astype(jnp.float32), precision=lax.Precision.HIGHEST, preferred_element_type=jnp.float32)


def pair_dot(first_pair, second_pair):
    real_real = wide_dot(first_pair[0], second_pair[0])
    imag_imag = wide_dot(first_pair[1], second_pair[1])
    real_imag = wide_dot(first_pair[0], second_pair[1])
    imag_real = wide_dot(first_pair[1], second_pair[0])
    return jnp.stack([real_real - imag_imag, real_imag + imag_real])


def kernel_rows(offsets, fractions):
    cells = jnp.arange(SUB, dtype=jnp.int32)[None, :] - offsets[:, None]
    distance = cells.astype(jnp.float32) - fractions[:, None] - (0.5 * KS - 1.0)
    inside = (cells >= 0) & (cells < KS)
    weights = jnp.where(inside, 0.5 * jnp.exp(-jnp.square(distance * (9.0 / KS))), 0.0)
    return weights.astype(jnp.bfloat16)


def subgrid_holder(worker):
    total_rows = worker.shape[0]
    slot_ids = jnp.arange(total_rows, dtype=jnp.int32)
    matches = (worker[None, :] == slot_ids[:, None]).astype(jnp.int32)
    return jnp.sum(matches * slot_ids[None, :], axis=1).astype(jnp.int32)


def adjoint_window(resid_grid, facet_id, facets):
    left_table = phase_table(facet_id, facets, True, -1.0)
    right_table = phase_table(jnp.mod(5 * facet_id + 3, facets), facets, False, -1.0)
    partial_value = pair_dot(left_table, resid_grid).astype(jnp.bfloat16)
    return pair_dot(partial_value, right_table).astype(jnp.bfloat16)


def reference(facet_spec, worker_of_subgrid, vis_count, bin_offsets, bin_fractions, observed):
    facets = facet_spec.shape[0]
    holder = subgrid_holder(worker_of_subgrid)
    facet_ids = jnp.arange(facets, dtype=jnp.int32)
    anchor = jnp.int32(0)

    def device_row(planes, device_id):
        subgrid = holder[device_id]
        top_row = ((subgrid // POS_V) * STEP).astype(jnp.int32)
        left_col = ((subgrid % POS_V) * STEP).astype(jnp.int32)

        def add_facet(running, facet_id):
            contribution = lax.dynamic_slice(facet_spec, (facet_id, anchor, top_row, left_col), (1, 2, MC, MC))[0]
            left_table = phase_table(facet_id, facets, False, 1.0)
            right_table = phase_table(jnp.mod(5 * facet_id + 3, facets), facets, True, 1.0)
            partial_value = pair_dot(left_table, contribution).astype(jnp.bfloat16)
            return running + pair_dot(partial_value, right_table), None

        grid_sum, _ = lax.scan(add_facet, jnp.zeros((2, SUB, SUB), jnp.float32), facet_ids)
        grid_half = grid_sum.astype(jnp.bfloat16)
        grid_cat = jnp.concatenate([grid_half[0], grid_half[1]], axis=1)
        offsets = bin_offsets[device_id]
        fractions = bin_fractions[device_id]
        observed_rows = observed[device_id]
        u_weights = kernel_rows(offsets[0], fractions[0])
        v_weights = kernel_rows(offsets[1], fractions[1])
        product = wide_dot(u_weights, grid_cat)
        v_float = v_weights.astype(jnp.float32)
        model_real = jnp.sum(product[:, :SUB] * v_float, axis=1)
        model_imag = jnp.sum(product[:, SUB:] * v_float, axis=1)
        live_mask = jnp.arange(VMAX, dtype=jnp.int32) < vis_count[device_id]
        real_part = jnp.where(live_mask, observed_rows[0] - model_real, 0.0)
        imag_part = jnp.where(live_mask, observed_rows[1] - model_imag, 0.0)
        weighted = jnp.concatenate([real_part[:, None] * v_float, imag_part[:, None] * v_float], axis=1).astype(jnp.bfloat16)
        gridded = lax.dot_general(u_weights.astype(jnp.float32), weighted.astype(jnp.float32), (((0,), (0,)), ((), ())), precision=lax.Precision.HIGHEST, preferred_element_type=jnp.float32)
        resid_grid = jnp.stack([gridded[:, :SUB], gridded[:, SUB:]]).astype(jnp.bfloat16)

        def one_window(facet_id):
            return adjoint_window(resid_grid, facet_id, facets)

        windows = lax.map(one_window, facet_ids)
        current = lax.dynamic_slice(planes, (anchor, anchor, top_row, left_col), (facets, 2, MC, MC))
        planes = lax.dynamic_update_slice(planes, current + windows.astype(jnp.float32), (anchor, anchor, top_row, left_col))
        return planes, jnp.stack([real_part, imag_part])

    planes, residual = lax.scan(device_row, jnp.zeros((facets, 2, PR, PC), jnp.float32), jnp.arange(SUBGRIDS, dtype=jnp.int32))
    return residual, planes
```

```python
import functools
import math

import jax
import jax.numpy as jnp
import numpy as np
from jax import lax
from jax.experimental import pallas as pl
from jax.experimental.pallas import tpu as pltpu
from jax.sharding import PartitionSpec as P

SUB = 256
MC = 256
STEP = 64
KS = 8
VB = 512
MESH = pl.DeviceIdType.MESH
VMEM = pl.BlockSpec(memory_space=pltpu.VMEM)
SMEM = pl.BlockSpec(memory_space=pltpu.SMEM)
F32 = jnp.float32
BF16 = jnp.bfloat16


def flip(index, bit):
    return index + bit - 2 * bit * ((index // bit) % 2)


def bits_of(count):
    return [1 << level for level in range(count.bit_length() - 1)]


def routes(count):
    bits = bits_of(count)
    return (bits, bits[:1] + bits[:0:-1])


def greet(count):
    me = lax.axis_index("facet")
    barrier = pltpu.get_barrier_semaphore()
    bits = bits_of(count)
    for bit in bits:
        pl.semaphore_signal(
            barrier, inc=1, device_id={"facet": flip(me, bit)}, device_id_type=MESH
        )
    pl.semaphore_wait(barrier, len(bits))


def remote(src, dst, send, recv, axis, target):
    return pltpu.make_async_remote_copy(
        src_ref=src,
        dst_ref=dst,
        send_sem=send,
        recv_sem=recv,
        device_id={axis: target},
        device_id_type=MESH,
    )


def transform_kernel(
    facets, pos_v, base, turns, worker, spec, slabs, left_adjoint, right_table,
    turned_table, corners, left_table, holder
):
    cols = spec.shape[3]
    pad = (pos_v - 1) * STEP
    me = lax.axis_index("facet")
    rank = lax.axis_index("sub")

    def note(subgrid, carry):
        holder[worker[subgrid]] = subgrid
        return carry

    lax.fori_loop(0, worker.shape[0], note, 0)
    for slab in range(facets):
        member = me
        for bit in bits_of(facets):
            member = flip(member, bit) if slab & bit else member
        subgrid = holder[member * pos_v + rank]
        corners[0, slab] = subgrid // pos_v * STEP
        corners[1, slab] = pad - subgrid % pos_v * STEP

    def turned(facet):
        turn = turns[facet]
        real, imag = turn[0:1], turn[1:2]
        return (base[0] * real - base[1] * imag, base[0] * imag + base[1] * real)

    real, imag = turned(me)
    left_adjoint[:MC, :SUB] = real.astype(BF16)
    left_adjoint[:MC, SUB:] = imag.astype(BF16)
    left_adjoint[MC:, :SUB] = (-imag).astype(BF16)
    left_adjoint[MC:, SUB:] = real.astype(BF16)
    real, imag = real.T, imag.T
    left_table[:SUB, :MC] = real.astype(BF16)
    left_table[:SUB, MC:] = (-imag).astype(BF16)
    left_table[SUB:, :MC] = imag.astype(BF16)
    left_table[SUB:, MC:] = real.astype(BF16)
    real, imag = turned((5 * me + 3) % facets)
    for table, first, second in ((right_table, real, imag), (turned_table, -imag, real)):
        table[:pad] = jnp.zeros((pad, 2 * SUB), BF16)
        table[pad + MC :] = jnp.zeros((pad, 2 * SUB), BF16)
        table[pad : pad + MC, :SUB] = first.astype(BF16)
        table[pad : pad + MC, SUB:] = second.astype(BF16)

    def transform(slab, carry):
        top = pl.multiple_of(corners[0, slab], STEP)
        left = pl.multiple_of(corners[1, slab], STEP)
        window = jnp.concatenate(
            [spec[0, 0, pl.ds(top, MC), :], spec[0, 1, pl.ds(top, MC), :]], axis=0
        )
        table = right_table[pl.ds(left, cols), :]
        mixed = jnp.dot(window, table, preferred_element_type=F32)
        real = mixed[:MC, :SUB] - mixed[MC:, SUB:]
        imag = mixed[:MC, SUB:] + mixed[MC:, :SUB]
        half = jnp.concatenate([real, imag], axis=0).astype(BF16)
        value = jnp.dot(left_table[...], half, preferred_element_type=F32)
        slabs[slab] = value.astype(BF16).reshape(2, SUB, SUB)
        return carry

    lax.fori_loop(0, facets, transform, 0, unroll=2)


def halve_kernel(facets, slabs, grid_out, total, landed, send, recv):
    me = lax.axis_index("facet")
    greet(facets)
    orders = routes(facets)
    levels = len(orders[0])
    sent = []

    def queue(part, level, held):
        rank = lambda slab: tuple(not slab & bit for bit in orders[part][level:])
        return sorted(held, key=rank)

    def copy_of(source, level, slab, part):
        bit = orders[part][level]
        return remote(
            source.at[slab, part], landed.at[level, slab - bit, part],
            send.at[2 * level + part, slab], recv.at[2 * level + part, slab - bit],
            "facet", flip(me, bit),
        )

    def post(source, level, slab, part):
        copy = copy_of(source, level, slab, part)
        copy.start()
        sent.append(copy)

    held = [list(range(facets))] * 2
    pairs = [queue(part, 0, [s for s in held[part] if s & 1]) for part in range(2)]
    for both in zip(*pairs):
        for part, slab in enumerate(both):
            post(slabs, 0, slab, part)
    for level in range(levels):
        held = [[s for s in held[p] if not s & orders[p][level]] for p in range(2)]
        pairs = [queue(part, level + 1, held[part]) for part in range(2)]
        for both in zip(*pairs):
            for part, slab in enumerate(both):
                copy_of(slabs, level, slab + orders[part][level], part).wait_recv()
                source = slabs if level == 0 else total
                value = source[slab, part].astype(F32) + landed[level, slab, part].astype(F32)
                if level == levels - 1:
                    grid_out[part] = value.astype(BF16)
                else:
                    total[slab, part] = value.astype(BF16)
                    if slab & orders[part][level + 1]:
                        post(total, level + 1, slab, part)
    for copy in sent:
        copy.wait_send()


def kernel_columns(offsets, fractions):
    cells = lax.broadcasted_iota(jnp.int32, (SUB, offsets.shape[1]), 0).astype(F32)
    scale = math.sqrt(math.log2(math.e)) * 9.0 / KS
    centred = cells - (offsets.astype(F32) + (0.5 * KS - 0.5))
    distance = centred * scale - (fractions - 0.5) * scale
    inside = jnp.abs(centred) < 0.5 * KS
    return jnp.where(inside, jnp.exp2(-1.0 - distance * distance), 0.0).astype(BF16)


def vis_kernel(count, grid, offsets, fractions, observed, residual, gridded, flipped, total):
    slots = offsets.shape[2]
    live_count = count[0]
    flipped[:SUB] = grid[0].astype(F32).T.astype(BF16)
    flipped[SUB:] = grid[1].astype(F32).T.astype(BF16)
    total[...] = jnp.zeros_like(total)
    residual[...] = jnp.zeros_like(residual)

    def half_block(first):
        span = pl.ds(first, VB)
        u_weights = kernel_columns(offsets[0, 0:1, span], fractions[0, 0:1, span])
        v_weights = kernel_columns(offsets[0, 1:2, span], fractions[0, 1:2, span])
        v_float = v_weights.astype(F32)
        product = jnp.dot(flipped[...], u_weights, preferred_element_type=F32)
        live = first + lax.broadcasted_iota(jnp.int32, (1, VB), 1) < live_count
        weighted = []
        for part in range(2):
            model = jnp.sum(product[part * SUB : (part + 1) * SUB] * v_float, axis=0, keepdims=True)
            row = jnp.where(live, observed[0, part : part + 1, span] - model, 0.0)
            residual[0, part : part + 1, span] = row
            weighted.append((row * v_float).astype(BF16))
        return lax.dot_general(
            u_weights,
            jnp.concatenate(weighted, axis=0),
            (((1,), (1,)), ((), ())),
            preferred_element_type=F32,
        )

    def block(index, carry):
        first = pl.multiple_of(index * 2 * VB, 2 * VB)
        total[...] += half_block(first) + half_block(first + VB)
        return carry

    lax.fori_loop(0, (live_count + 2 * VB - 1) // (2 * VB), block, 0)
    gridded[0] = total[:, :SUB].astype(BF16)
    gridded[1] = total[:, SUB:].astype(BF16)


def gather_kernel(facets, own, slabs, send, recv):
    me = lax.axis_index("facet")
    greet(facets)
    orders = [order[:0:-1] + order[:1] for order in routes(facets)]
    levels = len(orders[0])
    sent = []

    def copy_of(level, slab, part):
        bit = orders[part][level]
        source = slabs.at[slab, part] if slab else own.at[part]
        return remote(
            source, slabs.at[slab + bit, part],
            send.at[part, slab + bit], recv.at[part, slab + bit],
            "facet", flip(me, bit),
        )

    def post(level, slab, part):
        copy = copy_of(level, slab, part)
        copy.start()
        sent.append(copy)

    for level in range(levels):
        for part in range(2):
            post(level, 0, part)
    slabs[0] = own[...]
    held = [[0], [0]]
    for level in range(levels):
        for both in zip(*held):
            for part, slab in enumerate(both):
                copy_of(level, slab, part).wait_recv()
                for later in range(level + 1, levels):
                    post(later, slab + orders[part][level], part)
        held = [held[p] + [s + orders[p][level] for s in held[p]] for p in range(2)]
    for copy in sent:
        copy.wait_send()


def adjoint_kernel(facets, corners, everyone, left_table, right_table, turned_table, pieces, plane):
    cols = plane.shape[1] // 2
    chunk = pieces.shape[1]
    plane[...] = jnp.zeros_like(plane)

    def add_source(slab, carry):
        top = pl.multiple_of(corners[0, slab], STEP)
        left = pl.multiple_of(corners[1, slab], STEP)
        source = everyone[slab].reshape(2 * SUB, SUB)
        half = jnp.dot(left_table[...], source, preferred_element_type=F32)
        row = jnp.concatenate([half[:MC], half[MC:]], axis=1).astype(BF16)
        table = jnp.concatenate(
            [right_table[pl.ds(left, cols), :], turned_table[pl.ds(left, cols), :]], axis=0
        )
        window = lax.dot_general(row, table, (((1,), (1,)), ((), ())), preferred_element_type=F32)
        plane[pl.ds(top, MC), :] += window
        return carry

    lax.fori_loop(0, facets, add_source, 0, unroll=2)
    for piece in range(pieces.shape[0]):
        pieces[piece] = plane[piece * chunk : (piece + 1) * chunk, :].astype(BF16)


def line_kernel(groups, pieces, update, totals, landed, send, recv):
    me = lax.axis_index("sub")
    barrier = pltpu.get_barrier_semaphore()
    inner = (me > 0, me < groups - 1)
    ahead = ((me + 1) % groups, (me + groups - 1) % groups)
    behind = (ahead[1], ahead[0])
    for way in range(2):
        @pl.when(inner[way])
        def _():
            pl.semaphore_signal(
                barrier, inc=1, device_id={"sub": behind[way]}, device_id_type=MESH
            )
    between = jnp.logical_and(inner[0], inner[1])

    @pl.when(between)
    def _():
        pl.semaphore_wait(barrier, 2)

    @pl.when(jnp.logical_not(between))
    def _():
        pl.semaphore_wait(barrier, 1)

    cols = update.shape[3]
    size = pieces.shape[1]
    cut = (size // 2 + 15) // 16 * 16
    spans = (pl.ds(0, cut), pl.ds(cut, size - cut))

    def copy_of(source, way, chunk, part):
        return remote(
            source.at[chunk, spans[part]], landed.at[way, chunk, spans[part]],
            send.at[way, chunk, part], recv.at[way, chunk, part], "sub", ahead[way],
        )

    def plan(place):
        steps = []
        for way in range(2):
            depth = place if way == 0 else groups - 1 - place
            for turn in range(2 * (groups - 1 - depth)):
                chunk = turn // 2 if way else groups - 1 - turn // 2
                steps.append((turn + depth, depth, way, chunk, turn % 2))
        return sorted(steps)

    for place in range(groups):
        @pl.when(me == place)
        def _():
            for _, depth, way, chunk, part in plan(place):
                if depth == 0:
                    copy_of(pieces, way, chunk, part).start()
                    continue
                copy_of(pieces, way, chunk, part).wait_recv()
                totals[way, chunk, spans[part]] = (
                    pieces[chunk, spans[part]].astype(F32)
                    + landed[way, chunk, spans[part]].astype(F32)
                ).astype(BF16)
                copy_of(totals.at[way], way, chunk, part).start()
            for part in range(2):
                span = spans[part]
                value = pieces[place, span].astype(F32)
                for way in range(2):
                    if place != (0, groups - 1)[way]:
                        copy_of(pieces, way, place, part).wait_recv()
                        value = value + landed[way, place, span].astype(F32)
                update[0, 0, span] = value[:, :cols]
                update[0, 1, span] = value[:, cols:]
            for _, depth, way, chunk, part in plan(place):
                copy_of(pieces, way, chunk, part).wait_send()


def phases(facets):
    modulus = SUB * facets
    centred = np.arange(SUB) - SUB // 2
    base = np.exp(2j * np.pi * (np.outer(centred, centred) * facets % modulus) / modulus)
    turn = np.exp(2j * np.pi * (np.outer(np.arange(facets), centred) % modulus) / modulus)
    pair = lambda z: jnp.asarray(np.stack([z.real, z.imag]).astype(np.float32))
    return pair(base * MC ** (-0.5)), jnp.swapaxes(pair(turn), 0, 1)


def staged_path(facet_spec, worker_of_subgrid, vis_count, bin_offsets, bin_fractions, observed):
    facets = lax.axis_size("facet")
    pos_v = lax.axis_size("sub")
    rows = facet_spec.shape[2]
    cols = facet_spec.shape[3]
    pad = (pos_v - 1) * STEP
    slots = bin_offsets.shape[2]
    base, turns = phases(facets)
    levels = len(bits_of(facets))
    slab_shape = (2, SUB, SUB)
    limit = 60 * 1024 * 1024
    slabs, left_adjoint, right, right_turned, corners = pl.pallas_call(
        functools.partial(transform_kernel, facets, pos_v),
        out_shape=(
            jax.ShapeDtypeStruct((facets,) + slab_shape, BF16),
            jax.ShapeDtypeStruct((2 * MC, 2 * SUB), BF16),
            jax.ShapeDtypeStruct((MC + 2 * pad, 2 * SUB), BF16),
            jax.ShapeDtypeStruct((MC + 2 * pad, 2 * SUB), BF16),
            jax.ShapeDtypeStruct((2, facets), jnp.int32),
        ),
        in_specs=[VMEM, VMEM, SMEM, VMEM],
        out_specs=(VMEM, VMEM, VMEM, VMEM, SMEM),
        scratch_shapes=[
            pltpu.VMEM((2 * SUB, 2 * MC), BF16),
            pltpu.SMEM(worker_of_subgrid.shape, jnp.int32),
        ],
        compiler_params=pltpu.CompilerParams(vmem_limit_bytes=limit),
        name="transform",
    )(base, turns, worker_of_subgrid, facet_spec)

    grid = pl.pallas_call(
        functools.partial(halve_kernel, facets),
        out_shape=jax.ShapeDtypeStruct(slab_shape, BF16),
        in_specs=[VMEM],
        out_specs=VMEM,
        scratch_shapes=[
            pltpu.VMEM((facets,) + slab_shape, BF16),
            pltpu.VMEM((levels, facets) + slab_shape, BF16),
            pltpu.SemaphoreType.DMA((2 * levels, facets)),
            pltpu.SemaphoreType.DMA((2 * levels, facets)),
        ],
        compiler_params=pltpu.CompilerParams(
            collective_id=0, has_side_effects=True, vmem_limit_bytes=limit
        ),
        name="sum_grids",
    )(slabs)

    residual, gridded = pl.pallas_call(
        vis_kernel,
        out_shape=(
            jax.ShapeDtypeStruct((1, 2, slots), F32),
            jax.ShapeDtypeStruct(slab_shape, BF16),
        ),
        in_specs=[SMEM, VMEM, VMEM, VMEM, VMEM],
        out_specs=(VMEM, VMEM),
        scratch_shapes=[
            pltpu.VMEM((2 * SUB, SUB), BF16),
            pltpu.VMEM((SUB, 2 * SUB), F32),
        ],
        compiler_params=pltpu.CompilerParams(vmem_limit_bytes=limit),
        name="visibilities",
    )(vis_count, grid, bin_offsets, bin_fractions, observed)

    everyone = pl.pallas_call(
        functools.partial(gather_kernel, facets),
        out_shape=jax.ShapeDtypeStruct((facets,) + slab_shape, BF16),
        in_specs=[VMEM],
        out_specs=VMEM,
        scratch_shapes=[
            pltpu.SemaphoreType.DMA((2, facets)),
            pltpu.SemaphoreType.DMA((2, facets)),
        ],
        compiler_params=pltpu.CompilerParams(
            collective_id=1, has_side_effects=True, vmem_limit_bytes=limit
        ),
        name="gather_grids",
    )(gridded)

    chunk = rows // pos_v
    pieces = pl.pallas_call(
        functools.partial(adjoint_kernel, facets),
        out_shape=jax.ShapeDtypeStruct((pos_v, chunk, 2 * cols), BF16),
        in_specs=[SMEM, VMEM, VMEM, VMEM, VMEM],
        out_specs=VMEM,
        scratch_shapes=[pltpu.VMEM((rows, 2 * cols), F32)],
        compiler_params=pltpu.CompilerParams(vmem_limit_bytes=limit),
        name="adjoint",
    )(corners, everyone, left_adjoint, right, right_turned)

    update = pl.pallas_call(
        functools.partial(line_kernel, pos_v),
        out_shape=jax.ShapeDtypeStruct((1, 2, chunk, cols), F32),
        in_specs=[VMEM],
        out_specs=VMEM,
        scratch_shapes=[
            pltpu.VMEM((2, pos_v, chunk, 2 * cols), BF16),
            pltpu.VMEM((2, pos_v, chunk, 2 * cols), BF16),
            pltpu.SemaphoreType.DMA((2, pos_v, 2)),
            pltpu.SemaphoreType.DMA((2, pos_v, 2)),
        ],
        compiler_params=pltpu.CompilerParams(
            collective_id=2, has_side_effects=True, vmem_limit_bytes=limit
        ),
        name="sum_pieces",
    )(pieces)
    return (residual, update)


CELLS = 16
FILL = 4


def spread(values, groups):
    zero = jnp.zeros_like(values)
    rows = [jnp.where(groups == cell, values, zero) for cell in range(SUB // CELLS)]
    return jnp.concatenate(rows, axis=0)


def compact(offsets, fractions):
    row = lax.broadcasted_iota(jnp.int32, (CELLS, offsets.shape[1]), 0)
    ahead = (row - offsets) & (CELLS - 1)
    scale = math.sqrt(math.log2(math.e)) * 9.0 / KS
    distance = (ahead.astype(F32) - (0.5 * KS - 1.0) - fractions) * scale
    values = jnp.where(ahead < KS, jnp.exp2(-1.0 - distance * distance), 0.0)
    return values.astype(BF16), (offsets + ahead) // CELLS


def gather_cells(product, bits):
    parts = [product[i * CELLS : (i + 1) * CELLS] for i in range(SUB // CELLS)]
    for bit in bits:
        parts = [jnp.where(bit, b, a) for a, b in zip(parts[::2], parts[1::2])]
    return parts[0]


def row_spans(size):
    step = (size // FILL + 15) // 16 * 16
    return [(at, min(step, size - at)) for at in range(0, size, step)]


def corners_kernel(facets, pos_v, margin, worker, corners, holder):
    me = lax.axis_index("facet")
    rank = lax.axis_index("sub")

    def note(subgrid, carry):
        holder[worker[subgrid]] = subgrid
        return carry

    lax.fori_loop(0, worker.shape[0], note, 0, unroll=8)
    for slab in range(facets):
        member = me
        for bit in bits_of(facets):
            member = flip(member, bit) if slab & bit else member
        subgrid = holder[member * pos_v + rank]
        top, left = subgrid // pos_v, subgrid % pos_v
        corners[0, slab] = top
        corners[1, slab] = left
        corners[2, slab] = (margin - top * STEP) // CELLS


def fused_kernel(
    facets, pos_v, block, base, turns, corners, count, spec, offsets, fractions, observed,
    residual, update, left_table, right_table, placed_table, views, out_core, in_core,
    out_x, out_y, in_x, in_y, kept, grid, u_dense, v_values, v_groups, total, slabs, padded,
    staged, landed, core_sems, x_sems, y_sems, gather_sems, line_sems
):
    me = lax.axis_index("facet")
    rank = lax.axis_index("sub")
    cols, rows = spec.shape[2], spec.shape[3]
    slots = offsets.shape[2]
    margin = rows - MC
    core, axis_x, axis_y = 1, 2, 4
    here = {bit: flip(me, bit) for bit in (core, axis_x, axis_y)}

    barrier = pltpu.get_barrier_semaphore()
    for bit in here:
        pl.semaphore_signal(barrier, inc=1, device_id={"facet": here[bit]}, device_id_type=MESH)
    inner = (rank > 0, rank < pos_v - 1)
    ahead = ((rank + 1) % pos_v, (rank + pos_v - 1) % pos_v)
    for way in range(2):
        @pl.when(inner[way])
        def _():
            pl.semaphore_signal(
                barrier, inc=1, device_id={"sub": ahead[1 - way]}, device_id_type=MESH
            )

    def turned(facet):
        turn = turns[facet]
        real, imag = turn[0:1], turn[1:2]
        return (base[0] * real - base[1] * imag, base[0] * imag + base[1] * real)

    def quarters(table, real, imag, flipped_first):
        table[:MC, :SUB] = real.astype(BF16)
        table[MC:, SUB:] = real.astype(BF16)
        low, high = (-imag, imag) if flipped_first else (imag, -imag)
        table[:MC, SUB:] = low.astype(BF16)
        table[MC:, :SUB] = high.astype(BF16)

    real, imag = turned(me)
    quarters(left_table, real, imag, False)
    real, imag = turned((5 * me + 3) % facets)
    b_real, b_imag = real.T, imag.T
    quarters(right_table, b_real, b_imag, True)
    for part in range(2):
        even, odd = spec[0, part], spec[0, part, :, STEP:]
        for top in range(views.shape[0]):
            at = top // 2 * 2 * STEP
            view = (odd if top % 2 else even)[:, at : at + MC]
            views[top, part] = view.reshape(cols // STEP, STEP, MC)

    @pl.when(jnp.logical_and(inner[0], inner[1]))
    def _():
        pl.semaphore_wait(barrier, 5)

    @pl.when(jnp.logical_not(jnp.logical_and(inner[0], inner[1])))
    def _():
        pl.semaphore_wait(barrier, 4)

    sent = []

    def post(source, target, sems, index, bit):
        send, recv = sems
        copy = remote(source, target, send.at[index], recv.at[index], "facet", here[bit])
        copy.start()
        sent.append(copy)

    def arrive(source, target, sems, index, bit):
        send, recv = sems
        remote(source, target, send.at[index], recv.at[index], "facet", here[bit]).wait_recv()

    def contribution(slab):
        top, left = corners[0, slab], corners[1, slab]
        window = jnp.concatenate(
            [
                jnp.concatenate([views[top, part, left + i] for i in range(MC // STEP)], axis=0)
                for part in range(2)
            ],
            axis=1,
        )
        half = jnp.dot(window, left_table[...], preferred_element_type=F32).astype(BF16)
        half = jnp.concatenate([half[:, :SUB], half[:, SUB:]], axis=0)
        return jnp.dot(right_table[...], half, preferred_element_type=F32)

    def to_partner(slab):
        value = contribution(slab)
        out_core[slab // 2] = value.astype(BF16).reshape(2, SUB, SUB)
        post(out_core.at[slab // 2], in_core.at[slab // 2], core_sems, slab // 2, core)

    def own(slab):
        value = contribution(slab).reshape(2, SUB, SUB)
        arrive(out_core.at[slab // 2], in_core.at[slab // 2], core_sems, slab // 2, core)
        return value + in_core[slab // 2].astype(F32)

    def send_x(index, value):
        out_x[index] = value.astype(BF16)
        post(out_x.at[index], in_x.at[index], x_sems, index, axis_x)

    def send_y(index, value):
        out_y[index] = value.astype(BF16)
        post(out_y.at[index], in_y.at[index], y_sems, index, axis_y)

    def from_x(index):
        arrive(out_x.at[index], in_x.at[index], x_sems, index, axis_x)
        return in_x[index].astype(F32)

    def from_y(index):
        arrive(out_y.at[index], in_y.at[index], y_sems, index, axis_y)
        return in_y[index].astype(F32)

    to_partner(7)
    to_partner(3)
    to_partner(5)
    value = own(6)
    send_x(0, value[0])
    send_y(0, value[1])
    value = own(2)
    send_x(1, value[0])
    kept[0] = value[1]
    value = own(4)
    send_y(1, value[1])
    kept[1] = value[0]
    to_partner(1)
    value = own(0)
    kept[2] = value[0]
    kept[3] = value[1]

    def place(table, first, second):
        blank = jnp.zeros((SUB, cols * 2 - MC), F32)
        first = jnp.concatenate([first, blank], axis=1)
        second = pltpu.roll(jnp.concatenate([second, blank], axis=1), cols, 1)
        value = first + second
        for left in range(pos_v):
            moved = pltpu.roll(value, left * STEP, 1) if left else value
            placed_table[left, table * SUB : (table + 1) * SUB] = moved.astype(BF16)

    place(0, b_real, -b_imag)
    place(1, b_imag, b_real)
    send_x(2, kept[0] + from_y(0))
    send_y(2, kept[1] + from_x(0))

    def prepare(index, carry):
        span = pl.ds(pl.multiple_of(index * block, block), block)
        values, groups = compact(offsets[0, 0:1, span], fractions[0, 0:1, span])
        u_dense[:, span] = spread(values, groups.astype(jnp.int16))
        values, groups = compact(offsets[0, 1:2, span], fractions[0, 1:2, span])
        v_values[:, span] = values.astype(F32)
        v_groups[:, span] = groups
        return carry

    lax.fori_loop(0, slots // block, prepare, 0)

    def clear(slab, carry):
        blank = jnp.zeros((margin // CELLS, CELLS, 2 * cols), BF16)
        padded[slab, : margin // CELLS] = blank
        padded[slab, (margin + MC) // CELLS :] = blank
        return carry

    lax.fori_loop(0, facets, clear, 0)
    total[...] = jnp.zeros_like(total)

    grid[:SUB] = (kept[2] + from_x(1) + from_y(2)).astype(BF16)
    grid[SUB:] = (kept[3] + from_y(1) + from_x(2)).astype(BF16)

    live_count = count[0]

    def visit(index, carry):
        first = pl.multiple_of(index * block, block)
        span = pl.ds(first, block)
        u_weights = u_dense[:, span]
        values, groups = v_values[:, span], v_groups[:, span]
        short = groups.astype(jnp.int16)
        product = jnp.dot(grid[...], u_weights, preferred_element_type=F32)
        bits = [(groups & bit) != 0 for bit in bits_of(SUB // CELLS)]
        live = first + lax.broadcasted_iota(jnp.int32, (1, block), 1) < live_count
        weighted = []
        for part in range(2):
            cells = gather_cells(product[part * SUB : (part + 1) * SUB], bits)
            model = jnp.sum(cells * values, axis=0, keepdims=True)
            row = jnp.where(live, observed[0, part : part + 1, span] - model, 0.0)
            residual[0, part : part + 1, span] = row
            weighted.append(spread((row * values).astype(BF16), short))
        total[...] += lax.dot_general(
            u_weights,
            jnp.concatenate(weighted, axis=0),
            (((1,), (1,)), ((), ())),
            preferred_element_type=F32,
        )
        return carry

    lax.fori_loop(0, slots // block, visit, 0)
    for part in range(2):
        slabs[0, part] = total[:, part * SUB : (part + 1) * SUB].astype(BF16)

    def share(slab, part, bit):
        source, target = slabs.at[slab, part], slabs.at[slab + bit, part]
        send, recv = gather_sems
        copy = remote(
            source, target, send.at[slab + bit, part], recv.at[slab + bit, part],
            "facet", here[bit],
        )
        copy.start()
        sent.append(copy)

    def shared(slab, part):
        bit = slab & -slab
        send, recv = gather_sems
        remote(
            slabs.at[slab, part], slabs.at[slab, part], send.at[slab, part],
            recv.at[slab, part], "facet", here[bit],
        ).wait_recv()

    def adjoint(slab):
        source = slabs[slab].reshape(2 * SUB, SUB)
        half = jnp.dot(left_table[...], source, preferred_element_type=F32).astype(BF16)
        half = jnp.concatenate([half[:MC], half[MC:]], axis=1)
        window = jnp.dot(half, placed_table[corners[1, slab]], preferred_element_type=F32)
        window = window.astype(BF16).reshape(MC // CELLS, CELLS, 2 * cols)
        padded[slab, margin // CELLS : (margin + MC) // CELLS] = window

    share(0, 0, axis_x)
    share(0, 1, axis_y)
    share(0, 0, core)
    share(0, 1, core)
    share(0, 1, axis_x)
    share(0, 0, axis_y)
    adjoint(0)
    shared(1, 0)
    shared(1, 1)
    adjoint(1)
    shared(2, 0)
    share(2, 0, axis_y)
    share(2, 0, core)
    shared(4, 1)
    share(4, 1, axis_x)
    share(4, 1, core)
    shared(2, 1)
    share(2, 1, core)
    shared(4, 0)
    share(4, 0, core)
    adjoint(2)
    adjoint(4)
    shared(3, 0)
    shared(3, 1)
    adjoint(3)
    shared(6, 0)
    share(6, 0, core)
    shared(6, 1)
    share(6, 1, core)
    shared(5, 0)
    shared(5, 1)
    adjoint(5)
    adjoint(6)
    shared(7, 0)
    shared(7, 1)
    adjoint(7)

    piece = rows // pos_v
    spans = row_spans(piece)
    starts = [corners[2, slab] for slab in range(facets)]

    def own_rows(chunk, part):
        at, size = spans[part]
        value = jnp.zeros((size, 2 * cols), F32)
        for slab in range(facets):
            begin = starts[slab] + (chunk * piece + at) // CELLS
            pick = [padded[slab, begin + i] for i in range(size // CELLS)]
            value = value + jnp.concatenate(pick, axis=0).astype(F32)
        return value

    def line_copy(way, chunk, part):
        at, size = spans[part]
        send, recv = line_sems
        return remote(
            staged.at[chunk, pl.ds(at, size)], landed.at[way, chunk, pl.ds(at, size)],
            send.at[way, chunk, part], recv.at[way, chunk, part], "sub", ahead[way],
        )

    def plan(place):
        steps = []
        for way in range(2):
            depth = place if way == 0 else pos_v - 1 - place
            for turn in range(len(spans) * (pos_v - 1 - depth)):
                chunk = turn // len(spans)
                chunk = chunk if way else pos_v - 1 - chunk
                steps.append((turn + depth, depth, way, chunk, turn % len(spans)))
        return sorted(steps)

    for spot in range(pos_v):
        @pl.when(rank == spot)
        def _():
            for _, depth, way, chunk, part in plan(spot):
                at, size = spans[part]
                value = own_rows(chunk, part)
                if depth:
                    line_copy(way, chunk, part).wait_recv()
                    value = value + landed[way, chunk, pl.ds(at, size)].astype(F32)
                staged[chunk, pl.ds(at, size)] = value.astype(BF16)
                line_copy(way, chunk, part).start()
            for part, (at, size) in enumerate(spans):
                value = own_rows(spot, part)
                for way in range(2):
                    if spot != (0, pos_v - 1)[way]:
                        line_copy(way, spot, part).wait_recv()
                        value = value + landed[way, spot, pl.ds(at, size)].astype(F32)
                update[0, 0, pl.ds(at, size)] = value[:, :cols]
                update[0, 1, pl.ds(at, size)] = value[:, cols:]
            for _, depth, way, chunk, part in plan(spot):
                line_copy(way, chunk, part).wait_send()

    for copy in sent:
        copy.wait_send()


def fused(facet_spec, worker, vis_count, bin_offsets, bin_fractions, observed):
    facets = lax.axis_size("facet")
    pos_v = lax.axis_size("sub")
    rows, cols = facet_spec.shape[2:]
    slots = bin_offsets.shape[2]
    block = math.gcd(slots, 2048)
    base, turns = phases(facets)
    piece = rows // pos_v
    parts = len(row_spans(piece))
    dma = pltpu.SemaphoreType.DMA
    pair = lambda *shape: (dma(shape), dma(shape))
    corners = pl.pallas_call(
        functools.partial(corners_kernel, facets, pos_v, rows - MC),
        out_shape=jax.ShapeDtypeStruct((3, facets), jnp.int32),
        in_specs=[SMEM],
        out_specs=SMEM,
        scratch_shapes=[pltpu.SMEM(worker.shape, jnp.int32)],
        name="corners",
    )(worker)
    return pl.pallas_call(
        functools.partial(fused_kernel, facets, pos_v, block),
        out_shape=(
            jax.ShapeDtypeStruct((1, 2, slots), F32),
            jax.ShapeDtypeStruct((1, 2, piece, cols), F32),
        ),
        in_specs=[VMEM, VMEM, SMEM, SMEM, VMEM, VMEM, VMEM, VMEM],
        out_specs=(VMEM, VMEM),
        scratch_shapes=[
            pltpu.VMEM((2 * MC, 2 * SUB), BF16),
            pltpu.VMEM((2 * SUB, 2 * MC), BF16),
            pltpu.VMEM((pos_v, 2 * SUB, 2 * cols), BF16),
            pltpu.VMEM(((rows - MC) // STEP + 1, 2, cols // STEP, STEP, MC), BF16),
            pltpu.VMEM((facets // 2, 2, SUB, SUB), BF16),
            pltpu.VMEM((facets // 2, 2, SUB, SUB), BF16),
            pltpu.VMEM((3, SUB, SUB), BF16),
            pltpu.VMEM((3, SUB, SUB), BF16),
            pltpu.VMEM((3, SUB, SUB), BF16),
            pltpu.VMEM((3, SUB, SUB), BF16),
            pltpu.VMEM((4, SUB, SUB), F32),
            pltpu.VMEM((2 * SUB, SUB), BF16),
            pltpu.VMEM((SUB, slots), BF16),
            pltpu.VMEM((CELLS, slots), F32),
            pltpu.VMEM((CELLS, slots), jnp.int32),
            pltpu.VMEM((SUB, 2 * SUB), F32),
            pltpu.VMEM((facets, 2, SUB, SUB), BF16),
            pltpu.VMEM((facets, (2 * rows - MC) // CELLS, CELLS, 2 * cols), BF16),
            pltpu.VMEM((pos_v, piece, 2 * cols), BF16),
            pltpu.VMEM((2, pos_v, piece, 2 * cols), BF16),
            pair(facets // 2),
            pair(3),
            pair(3),
            pair(facets, 2),
            pair(2, pos_v, parts),
        ],
        compiler_params=pltpu.CompilerParams(
            collective_id=3, has_side_effects=True, vmem_limit_bytes=60 * 1024 * 1024
        ),
        name="everything",
    )(
        base, turns, corners, vis_count, jnp.swapaxes(facet_spec, 2, 3),
        bin_offsets, bin_fractions, observed,
    )


def on_device(facet_spec, *rest):
    facets = lax.axis_size("facet")
    rows, cols = facet_spec.shape[2:]
    padded_bytes = facets * (2 * rows - MC) * 2 * cols * 2
    fits = len(bits_of(facets)) == 3 and padded_bytes <= 20 * 1024 * 1024
    return (fused if fits else staged_path)(facet_spec, *rest)


def solution(mesh):
    placed = (
        P("facet", None, None, None),
        P(),
        P(("facet", "sub")),
        P(("facet", "sub"), None, None),
        P(("facet", "sub"), None, None),
        P(("facet", "sub"), None, None),
    )
    return jax.shard_map(
        on_device,
        mesh=mesh,
        in_specs=placed,
        out_specs=(P(("facet", "sub"), None, None), P("facet", None, "sub", None)),
        check_vma=False,
    )
```

```python
import functools
import math

import jax
import jax.numpy as jnp
import numpy as np
from jax import lax
from jax.experimental import pallas as pl
from jax.experimental.pallas import tpu as pltpu
from jax.sharding import PartitionSpec as P

SUB = 256
MC = 256
STEP = 64
KS = 8
VB = 512
MESH = pl.DeviceIdType.MESH
VMEM = pl.BlockSpec(memory_space=pltpu.VMEM)
SMEM = pl.BlockSpec(memory_space=pltpu.SMEM)
F32 = jnp.float32
BF16 = jnp.bfloat16


def flip(index, bit):
    return index + bit - 2 * bit * ((index // bit) % 2)


def bits_of(count):
    return [1 << level for level in range(count.bit_length() - 1)]


def routes(count):
    bits = bits_of(count)
    return (bits, bits[:1] + bits[:0:-1])


def greet(count):
    me = lax.axis_index("facet")
    barrier = pltpu.get_barrier_semaphore()
    bits = bits_of(count)
    for bit in bits:
        pl.semaphore_signal(
            barrier, inc=1, device_id={"facet": flip(me, bit)}, device_id_type=MESH
        )
    pl.semaphore_wait(barrier, len(bits))


def remote(src, dst, send, recv, axis, target):
    return pltpu.make_async_remote_copy(
        src_ref=src,
        dst_ref=dst,
        send_sem=send,
        recv_sem=recv,
        device_id={axis: target},
        device_id_type=MESH,
    )


def transform_kernel(
    facets, pos_v, base, turns, worker, spec, slabs, left_adjoint, right_table,
    turned_table, corners, left_table, holder
):
    cols = spec.shape[3]
    pad = (pos_v - 1) * STEP
    me = lax.axis_index("facet")
    rank = lax.axis_index("sub")

    def note(subgrid, carry):
        holder[worker[subgrid]] = subgrid
        return carry

    lax.fori_loop(0, worker.shape[0], note, 0)
    for slab in range(facets):
        member = me
        for bit in bits_of(facets):
            member = flip(member, bit) if slab & bit else member
        subgrid = holder[member * pos_v + rank]
        corners[0, slab] = subgrid // pos_v * STEP
        corners[1, slab] = pad - subgrid % pos_v * STEP

    def turned(facet):
        turn = turns[facet]
        real, imag = turn[0:1], turn[1:2]
        return (base[0] * real - base[1] * imag, base[0] * imag + base[1] * real)

    real, imag = turned(me)
    left_adjoint[:MC, :SUB] = real.astype(BF16)
    left_adjoint[:MC, SUB:] = imag.astype(BF16)
    left_adjoint[MC:, :SUB] = (-imag).astype(BF16)
    left_adjoint[MC:, SUB:] = real.astype(BF16)
    real, imag = real.T, imag.T
    left_table[:SUB, :MC] = real.astype(BF16)
    left_table[:SUB, MC:] = (-imag).astype(BF16)
    left_table[SUB:, :MC] = imag.astype(BF16)
    left_table[SUB:, MC:] = real.astype(BF16)
    real, imag = turned((5 * me + 3) % facets)
    for table, first, second in ((right_table, real, imag), (turned_table, -imag, real)):
        table[:pad] = jnp.zeros((pad, 2 * SUB), BF16)
        table[pad + MC :] = jnp.zeros((pad, 2 * SUB), BF16)
        table[pad : pad + MC, :SUB] = first.astype(BF16)
        table[pad : pad + MC, SUB:] = second.astype(BF16)

    def transform(slab, carry):
        top = pl.multiple_of(corners[0, slab], STEP)
        left = pl.multiple_of(corners[1, slab], STEP)
        window = jnp.concatenate(
            [spec[0, 0, pl.ds(top, MC), :], spec[0, 1, pl.ds(top, MC), :]], axis=0
        )
        table = right_table[pl.ds(left, cols), :]
        mixed = jnp.dot(window, table, preferred_element_type=F32)
        real = mixed[:MC, :SUB] - mixed[MC:, SUB:]
        imag = mixed[:MC, SUB:] + mixed[MC:, :SUB]
        half = jnp.concatenate([real, imag], axis=0).astype(BF16)
        value = jnp.dot(left_table[...], half, preferred_element_type=F32)
        slabs[slab] = value.astype(BF16).reshape(2, SUB, SUB)
        return carry

    lax.fori_loop(0, facets, transform, 0, unroll=2)


def halve_kernel(facets, slabs, grid_out, total, landed, send, recv):
    me = lax.axis_index("facet")
    greet(facets)
    orders = routes(facets)
    levels = len(orders[0])
    sent = []

    def queue(part, level, held):
        rank = lambda slab: tuple(not slab & bit for bit in orders[part][level:])
        return sorted(held, key=rank)

    def copy_of(source, level, slab, part):
        bit = orders[part][level]
        return remote(
            source.at[slab, part], landed.at[level, slab - bit, part],
            send.at[2 * level + part, slab], recv.at[2 * level + part, slab - bit],
            "facet", flip(me, bit),
        )

    def post(source, level, slab, part):
        copy = copy_of(source, level, slab, part)
        copy.start()
        sent.append(copy)

    held = [list(range(facets))] * 2
    pairs = [queue(part, 0, [s for s in held[part] if s & 1]) for part in range(2)]
    for both in zip(*pairs):
        for part, slab in enumerate(both):
            post(slabs, 0, slab, part)
    for level in range(levels):
        held = [[s for s in held[p] if not s & orders[p][level]] for p in range(2)]
        pairs = [queue(part, level + 1, held[part]) for part in range(2)]
        for both in zip(*pairs):
            for part, slab in enumerate(both):
                copy_of(slabs, level, slab + orders[part][level], part).wait_recv()
                source = slabs if level == 0 else total
                value = source[slab, part].astype(F32) + landed[level, slab, part].astype(F32)
                if level == levels - 1:
                    grid_out[part] = value.astype(BF16)
                else:
                    total[slab, part] = value.astype(BF16)
                    if slab & orders[part][level + 1]:
                        post(total, level + 1, slab, part)
    for copy in sent:
        copy.wait_send()


def kernel_columns(offsets, fractions):
    cells = lax.broadcasted_iota(jnp.int32, (SUB, offsets.shape[1]), 0).astype(F32)
    scale = math.sqrt(math.log2(math.e)) * 9.0 / KS
    centred = cells - (offsets.astype(F32) + (0.5 * KS - 0.5))
    distance = centred * scale - (fractions - 0.5) * scale
    inside = jnp.abs(centred) < 0.5 * KS
    return jnp.where(inside, jnp.exp2(-1.0 - distance * distance), 0.0).astype(BF16)


def vis_kernel(count, grid, offsets, fractions, observed, residual, gridded, flipped, total):
    slots = offsets.shape[2]
    live_count = count[0]
    flipped[:SUB] = grid[0].astype(F32).T.astype(BF16)
    flipped[SUB:] = grid[1].astype(F32).T.astype(BF16)
    total[...] = jnp.zeros_like(total)
    residual[...] = jnp.zeros_like(residual)

    def half_block(first):
        span = pl.ds(first, VB)
        u_weights = kernel_columns(offsets[0, 0:1, span], fractions[0, 0:1, span])
        v_weights = kernel_columns(offsets[0, 1:2, span], fractions[0, 1:2, span])
        v_float = v_weights.astype(F32)
        product = jnp.dot(flipped[...], u_weights, preferred_element_type=F32)
        live = first + lax.broadcasted_iota(jnp.int32, (1, VB), 1) < live_count
        weighted = []
        for part in range(2):
            model = jnp.sum(product[part * SUB : (part + 1) * SUB] * v_float, axis=0, keepdims=True)
            row = jnp.where(live, observed[0, part : part + 1, span] - model, 0.0)
            residual[0, part : part + 1, span] = row
            weighted.append((row * v_float).astype(BF16))
        return lax.dot_general(
            u_weights,
            jnp.concatenate(weighted, axis=0),
            (((1,), (1,)), ((), ())),
            preferred_element_type=F32,
        )

    def block(index, carry):
        first = pl.multiple_of(index * 2 * VB, 2 * VB)
        total[...] += half_block(first) + half_block(first + VB)
        return carry

    lax.fori_loop(0, (live_count + 2 * VB - 1) // (2 * VB), block, 0)
    gridded[0] = total[:, :SUB].astype(BF16)
    gridded[1] = total[:, SUB:].astype(BF16)


def gather_kernel(facets, own, slabs, send, recv):
    me = lax.axis_index("facet")
    greet(facets)
    orders = [order[:0:-1] + order[:1] for order in routes(facets)]
    levels = len(orders[0])
    sent = []

    def copy_of(level, slab, part):
        bit = orders[part][level]
        source = slabs.at[slab, part] if slab else own.at[part]
        return remote(
            source, slabs.at[slab + bit, part],
            send.at[part, slab + bit], recv.at[part, slab + bit],
            "facet", flip(me, bit),
        )

    def post(level, slab, part):
        copy = copy_of(level, slab, part)
        copy.start()
        sent.append(copy)

    for level in range(levels):
        for part in range(2):
            post(level, 0, part)
    slabs[0] = own[...]
    held = [[0], [0]]
    for level in range(levels):
        for both in zip(*held):
            for part, slab in enumerate(both):
                copy_of(level, slab, part).wait_recv()
                for later in range(level + 1, levels):
                    post(later, slab + orders[part][level], part)
        held = [held[p] + [s + orders[p][level] for s in held[p]] for p in range(2)]
    for copy in sent:
        copy.wait_send()


def adjoint_kernel(facets, corners, everyone, left_table, right_table, turned_table, pieces, plane):
    cols = plane.shape[1] // 2
    chunk = pieces.shape[1]
    plane[...] = jnp.zeros_like(plane)

    def add_source(slab, carry):
        top = pl.multiple_of(corners[0, slab], STEP)
        left = pl.multiple_of(corners[1, slab], STEP)
        source = everyone[slab].reshape(2 * SUB, SUB)
        half = jnp.dot(left_table[...], source, preferred_element_type=F32)
        row = jnp.concatenate([half[:MC], half[MC:]], axis=1).astype(BF16)
        table = jnp.concatenate(
            [right_table[pl.ds(left, cols), :], turned_table[pl.ds(left, cols), :]], axis=0
        )
        window = lax.dot_general(row, table, (((1,), (1,)), ((), ())), preferred_element_type=F32)
        plane[pl.ds(top, MC), :] += window
        return carry

    lax.fori_loop(0, facets, add_source, 0, unroll=2)
    for piece in range(pieces.shape[0]):
        pieces[piece] = plane[piece * chunk : (piece + 1) * chunk, :].astype(BF16)


def line_kernel(groups, pieces, update, totals, landed, send, recv):
    me = lax.axis_index("sub")
    barrier = pltpu.get_barrier_semaphore()
    inner = (me > 0, me < groups - 1)
    ahead = ((me + 1) % groups, (me + groups - 1) % groups)
    behind = (ahead[1], ahead[0])
    for way in range(2):
        @pl.when(inner[way])
        def _():
            pl.semaphore_signal(
                barrier, inc=1, device_id={"sub": behind[way]}, device_id_type=MESH
            )
    between = jnp.logical_and(inner[0], inner[1])

    @pl.when(between)
    def _():
        pl.semaphore_wait(barrier, 2)

    @pl.when(jnp.logical_not(between))
    def _():
        pl.semaphore_wait(barrier, 1)

    cols = update.shape[3]
    size = pieces.shape[1]
    cut = (size // 2 + 15) // 16 * 16
    spans = (pl.ds(0, cut), pl.ds(cut, size - cut))

    def copy_of(source, way, chunk, part):
        return remote(
            source.at[chunk, spans[part]], landed.at[way, chunk, spans[part]],
            send.at[way, chunk, part], recv.at[way, chunk, part], "sub", ahead[way],
        )

    def plan(place):
        steps = []
        for way in range(2):
            depth = place if way == 0 else groups - 1 - place
            for turn in range(2 * (groups - 1 - depth)):
                chunk = turn // 2 if way else groups - 1 - turn // 2
                steps.append((turn + depth, depth, way, chunk, turn % 2))
        return sorted(steps)

    for place in range(groups):
        @pl.when(me == place)
        def _():
            for _, depth, way, chunk, part in plan(place):
                if depth == 0:
                    copy_of(pieces, way, chunk, part).start()
                    continue
                copy_of(pieces, way, chunk, part).wait_recv()
                totals[way, chunk, spans[part]] = (
                    pieces[chunk, spans[part]].astype(F32)
                    + landed[way, chunk, spans[part]].astype(F32)
                ).astype(BF16)
                copy_of(totals.at[way], way, chunk, part).start()
            for part in range(2):
                span = spans[part]
                value = pieces[place, span].astype(F32)
                for way in range(2):
                    if place != (0, groups - 1)[way]:
                        copy_of(pieces, way, place, part).wait_recv()
                        value = value + landed[way, place, span].astype(F32)
                update[0, 0, span] = value[:, :cols]
                update[0, 1, span] = value[:, cols:]
            for _, depth, way, chunk, part in plan(place):
                copy_of(pieces, way, chunk, part).wait_send()


def phases(facets):
    modulus = SUB * facets
    centred = np.arange(SUB) - SUB // 2
    base = np.exp(2j * np.pi * (np.outer(centred, centred) * facets % modulus) / modulus)
    turn = np.exp(2j * np.pi * (np.outer(np.arange(facets), centred) % modulus) / modulus)
    pair = lambda z: jnp.asarray(np.stack([z.real, z.imag]).astype(np.float32))
    return pair(base * MC ** (-0.5)), jnp.swapaxes(pair(turn), 0, 1)


def staged_path(facet_spec, worker_of_subgrid, vis_count, bin_offsets, bin_fractions, observed):
    facets = lax.axis_size("facet")
    pos_v = lax.axis_size("sub")
    rows = facet_spec.shape[2]
    cols = facet_spec.shape[3]
    pad = (pos_v - 1) * STEP
    slots = bin_offsets.shape[2]
    base, turns = phases(facets)
    levels = len(bits_of(facets))
    slab_shape = (2, SUB, SUB)
    limit = 60 * 1024 * 1024
    slabs, left_adjoint, right, right_turned, corners = pl.pallas_call(
        functools.partial(transform_kernel, facets, pos_v),
        out_shape=(
            jax.ShapeDtypeStruct((facets,) + slab_shape, BF16),
            jax.ShapeDtypeStruct((2 * MC, 2 * SUB), BF16),
            jax.ShapeDtypeStruct((MC + 2 * pad, 2 * SUB), BF16),
            jax.ShapeDtypeStruct((MC + 2 * pad, 2 * SUB), BF16),
            jax.ShapeDtypeStruct((2, facets), jnp.int32),
        ),
        in_specs=[VMEM, VMEM, SMEM, VMEM],
        out_specs=(VMEM, VMEM, VMEM, VMEM, SMEM),
        scratch_shapes=[
            pltpu.VMEM((2 * SUB, 2 * MC), BF16),
            pltpu.SMEM(worker_of_subgrid.shape, jnp.int32),
        ],
        compiler_params=pltpu.CompilerParams(vmem_limit_bytes=limit),
        name="transform",
    )(base, turns, worker_of_subgrid, facet_spec)

    grid = pl.pallas_call(
        functools.partial(halve_kernel, facets),
        out_shape=jax.ShapeDtypeStruct(slab_shape, BF16),
        in_specs=[VMEM],
        out_specs=VMEM,
        scratch_shapes=[
            pltpu.VMEM((facets,) + slab_shape, BF16),
            pltpu.VMEM((levels, facets) + slab_shape, BF16),
            pltpu.SemaphoreType.DMA((2 * levels, facets)),
            pltpu.SemaphoreType.DMA((2 * levels, facets)),
        ],
        compiler_params=pltpu.CompilerParams(
            collective_id=0, has_side_effects=True, vmem_limit_bytes=limit
        ),
        name="sum_grids",
    )(slabs)

    residual, gridded = pl.pallas_call(
        vis_kernel,
        out_shape=(
            jax.ShapeDtypeStruct((1, 2, slots), F32),
            jax.ShapeDtypeStruct(slab_shape, BF16),
        ),
        in_specs=[SMEM, VMEM, VMEM, VMEM, VMEM],
        out_specs=(VMEM, VMEM),
        scratch_shapes=[
            pltpu.VMEM((2 * SUB, SUB), BF16),
            pltpu.VMEM((SUB, 2 * SUB), F32),
        ],
        compiler_params=pltpu.CompilerParams(vmem_limit_bytes=limit),
        name="visibilities",
    )(vis_count, grid, bin_offsets, bin_fractions, observed)

    everyone = pl.pallas_call(
        functools.partial(gather_kernel, facets),
        out_shape=jax.ShapeDtypeStruct((facets,) + slab_shape, BF16),
        in_specs=[VMEM],
        out_specs=VMEM,
        scratch_shapes=[
            pltpu.SemaphoreType.DMA((2, facets)),
            pltpu.SemaphoreType.DMA((2, facets)),
        ],
        compiler_params=pltpu.CompilerParams(
            collective_id=1, has_side_effects=True, vmem_limit_bytes=limit
        ),
        name="gather_grids",
    )(gridded)

    chunk = rows // pos_v
    pieces = pl.pallas_call(
        functools.partial(adjoint_kernel, facets),
        out_shape=jax.ShapeDtypeStruct((pos_v, chunk, 2 * cols), BF16),
        in_specs=[SMEM, VMEM, VMEM, VMEM, VMEM],
        out_specs=VMEM,
        scratch_shapes=[pltpu.VMEM((rows, 2 * cols), F32)],
        compiler_params=pltpu.CompilerParams(vmem_limit_bytes=limit),
        name="adjoint",
    )(corners, everyone, left_adjoint, right, right_turned)

    update = pl.pallas_call(
        functools.partial(line_kernel, pos_v),
        out_shape=jax.ShapeDtypeStruct((1, 2, chunk, cols), F32),
        in_specs=[VMEM],
        out_specs=VMEM,
        scratch_shapes=[
            pltpu.VMEM((2, pos_v, chunk, 2 * cols), BF16),
            pltpu.VMEM((2, pos_v, chunk, 2 * cols), BF16),
            pltpu.SemaphoreType.DMA((2, pos_v, 2)),
            pltpu.SemaphoreType.DMA((2, pos_v, 2)),
        ],
        compiler_params=pltpu.CompilerParams(
            collective_id=2, has_side_effects=True, vmem_limit_bytes=limit
        ),
        name="sum_pieces",
    )(pieces)
    return (residual, update)


CELLS = 16
FILL = 4


def spread(values, groups):
    zero = jnp.zeros_like(values)
    rows = [jnp.where(groups == cell, values, zero) for cell in range(SUB // CELLS)]
    return jnp.concatenate(rows, axis=0)


def compact(offsets, fractions):
    row = lax.broadcasted_iota(jnp.int32, (CELLS, offsets.shape[1]), 0)
    ahead = (row - offsets) & (CELLS - 1)
    scale = math.sqrt(math.log2(math.e)) * 9.0 / KS
    distance = (ahead.astype(F32) - (0.5 * KS - 1.0) - fractions) * scale
    values = jnp.where(ahead < KS, jnp.exp2(-1.0 - distance * distance), 0.0)
    return values.astype(BF16), (offsets + ahead) // CELLS


def gather_cells(product, bits):
    parts = [product[i * CELLS : (i + 1) * CELLS] for i in range(SUB // CELLS)]
    for bit in bits:
        parts = [jnp.where(bit, b, a) for a, b in zip(parts[::2], parts[1::2])]
    return parts[0]


def row_spans(size):
    step = (size // FILL + 15) // 16 * 16
    return [(at, min(step, size - at)) for at in range(0, size, step)]


def fused_kernel(
    facets, pos_v, block, base, turns, worker, count, spec, offsets, fractions, observed,
    residual, update, left_table, right_table, placed_table, views, out_core, in_core,
    out_x, out_y, in_x, in_y, kept, grid, u_dense, v_values, v_groups, total, slabs, padded,
    staged, landed, core_sems, x_sems, y_sems, gather_sems, line_sems
):
    me = lax.axis_index("facet")
    rank = lax.axis_index("sub")
    cols, rows = spec.shape[2], spec.shape[3]
    slots = offsets.shape[2]
    margin = rows - MC
    core, axis_x, axis_y = 1, 2, 4
    here = {bit: flip(me, bit) for bit in (core, axis_x, axis_y)}

    barrier = pltpu.get_barrier_semaphore()
    for bit in here:
        pl.semaphore_signal(barrier, inc=1, device_id={"facet": here[bit]}, device_id_type=MESH)
    inner = (rank > 0, rank < pos_v - 1)
    ahead = ((rank + 1) % pos_v, (rank + pos_v - 1) % pos_v)
    for way in range(2):
        @pl.when(inner[way])
        def _():
            pl.semaphore_signal(
                barrier, inc=1, device_id={"sub": ahead[1 - way]}, device_id_type=MESH
            )

    wanted = []
    for slab in range(facets):
        member = me
        for bit in bits_of(facets):
            member = flip(member, bit) if slab & bit else member
        wanted.append(member * pos_v + rank)

    def note(subgrid, found):
        at = worker[subgrid]
        return tuple(jnp.where(at == w, subgrid, f) for w, f in zip(wanted, found))

    found = lax.fori_loop(
        0, worker.shape[0], note, tuple(jnp.int32(0) for _ in wanted), unroll=8
    )
    tops = [subgrid // pos_v for subgrid in found]
    lefts = [subgrid % pos_v for subgrid in found]

    def turned(facet):
        turn = turns[facet]
        real, imag = turn[0:1], turn[1:2]
        return (base[0] * real - base[1] * imag, base[0] * imag + base[1] * real)

    def quarters(table, real, imag, flipped_first):
        table[:MC, :SUB] = real.astype(BF16)
        table[MC:, SUB:] = real.astype(BF16)
        low, high = (-imag, imag) if flipped_first else (imag, -imag)
        table[:MC, SUB:] = low.astype(BF16)
        table[MC:, :SUB] = high.astype(BF16)

    real, imag = turned(me)
    quarters(left_table, real, imag, False)
    real, imag = turned((5 * me + 3) % facets)
    b_real, b_imag = real.T, imag.T
    quarters(right_table, b_real, b_imag, True)
    for part in range(2):
        even, odd = spec[0, part], spec[0, part, :, STEP:]
        for top in range(views.shape[0]):
            at = top // 2 * 2 * STEP
            view = (odd if top % 2 else even)[:, at : at + MC]
            views[top, part] = view.reshape(cols // STEP, STEP, MC)

    @pl.when(jnp.logical_and(inner[0], inner[1]))
    def _():
        pl.semaphore_wait(barrier, 5)

    @pl.when(jnp.logical_not(jnp.logical_and(inner[0], inner[1])))
    def _():
        pl.semaphore_wait(barrier, 4)

    sent = []

    def post(source, target, sems, index, bit):
        send, recv = sems
        copy = remote(source, target, send.at[index], recv.at[index], "facet", here[bit])
        copy.start()
        sent.append(copy)

    def arrive(source, target, sems, index, bit):
        send, recv = sems
        remote(source, target, send.at[index], recv.at[index], "facet", here[bit]).wait_recv()

    def contribution(slab):
        top, left = tops[slab], lefts[slab]
        window = jnp.concatenate(
            [
                jnp.concatenate([views[top, part, left + i] for i in range(MC // STEP)], axis=0)
                for part in range(2)
            ],
            axis=1,
        )
        half = jnp.dot(window, left_table[...], preferred_element_type=F32).astype(BF16)
        half = jnp.concatenate([half[:, :SUB], half[:, SUB:]], axis=0)
        return jnp.dot(right_table[...], half, preferred_element_type=F32)

    def to_partner(slab):
        value = contribution(slab)
        out_core[slab // 2] = value.astype(BF16).reshape(2, SUB, SUB)
        post(out_core.at[slab // 2], in_core.at[slab // 2], core_sems, slab // 2, core)

    def own(slab):
        value = contribution(slab).reshape(2, SUB, SUB)
        arrive(out_core.at[slab // 2], in_core.at[slab // 2], core_sems, slab // 2, core)
        return value + in_core[slab // 2].astype(F32)

    def send_x(index, value):
        out_x[index] = value.astype(BF16)
        post(out_x.at[index], in_x.at[index], x_sems, index, axis_x)

    def send_y(index, value):
        out_y[index] = value.astype(BF16)
        post(out_y.at[index], in_y.at[index], y_sems, index, axis_y)

    def from_x(index):
        arrive(out_x.at[index], in_x.at[index], x_sems, index, axis_x)
        return in_x[index].astype(F32)

    def from_y(index):
        arrive(out_y.at[index], in_y.at[index], y_sems, index, axis_y)
        return in_y[index].astype(F32)

    to_partner(7)
    to_partner(3)
    to_partner(5)
    value = own(6)
    send_x(0, value[0])
    send_y(0, value[1])
    value = own(2)
    send_x(1, value[0])
    kept[0] = value[1]
    value = own(4)
    send_y(1, value[1])
    kept[1] = value[0]
    to_partner(1)
    value = own(0)
    kept[2] = value[0]
    kept[3] = value[1]

    def place(table, first, second):
        blank = jnp.zeros((SUB, cols * 2 - MC), F32)
        first = jnp.concatenate([first, blank], axis=1)
        second = pltpu.roll(jnp.concatenate([second, blank], axis=1), cols, 1)
        value = first + second
        for left in range(pos_v):
            moved = pltpu.roll(value, left * STEP, 1) if left else value
            placed_table[left, table * SUB : (table + 1) * SUB] = moved.astype(BF16)

    place(0, b_real, -b_imag)
    place(1, b_imag, b_real)
    send_x(2, kept[0] + from_y(0))
    send_y(2, kept[1] + from_x(0))

    def prepare(index, carry):
        span = pl.ds(pl.multiple_of(index * block, block), block)
        values, groups = compact(offsets[0, 0:1, span], fractions[0, 0:1, span])
        u_dense[:, span] = spread(values, groups.astype(jnp.int16))
        values, groups = compact(offsets[0, 1:2, span], fractions[0, 1:2, span])
        v_values[:, span] = values.astype(F32)
        v_groups[:, span] = groups
        return carry

    lax.fori_loop(0, slots // block, prepare, 0)

    def clear(slab, carry):
        blank = jnp.zeros((margin // CELLS, CELLS, 2 * cols), BF16)
        padded[slab, : margin // CELLS] = blank
        padded[slab, (margin + MC) // CELLS :] = blank
        return carry

    lax.fori_loop(0, facets, clear, 0)
    total[...] = jnp.zeros_like(total)

    grid[:SUB] = (kept[2] + from_x(1) + from_y(2)).astype(BF16)
    grid[SUB:] = (kept[3] + from_y(1) + from_x(2)).astype(BF16)

    live_count = count[0]

    def visit(index, carry):
        first = pl.multiple_of(index * block, block)
        span = pl.ds(first, block)
        u_weights = u_dense[:, span]
        values, groups = v_values[:, span], v_groups[:, span]
        short = groups.astype(jnp.int16)
        product = jnp.dot(grid[...], u_weights, preferred_element_type=F32)
        bits = [(groups & bit) != 0 for bit in bits_of(SUB // CELLS)]
        live = first + lax.broadcasted_iota(jnp.int32, (1, block), 1) < live_count
        weighted = []
        for part in range(2):
            cells = gather_cells(product[part * SUB : (part + 1) * SUB], bits)
            model = jnp.sum(cells * values, axis=0, keepdims=True)
            row = jnp.where(live, observed[0, part : part + 1, span] - model, 0.0)
            residual[0, part : part + 1, span] = row
            weighted.append(spread((row * values).astype(BF16), short))
        total[...] += lax.dot_general(
            u_weights,
            jnp.concatenate(weighted, axis=0),
            (((1,), (1,)), ((), ())),
            preferred_element_type=F32,
        )
        return carry

    lax.fori_loop(0, slots // block, visit, 0)
    for part in range(2):
        slabs[0, part] = total[:, part * SUB : (part + 1) * SUB].astype(BF16)

    def share(slab, part, bit):
        source, target = slabs.at[slab, part], slabs.at[slab + bit, part]
        send, recv = gather_sems
        copy = remote(
            source, target, send.at[slab + bit, part], recv.at[slab + bit, part],
            "facet", here[bit],
        )
        copy.start()
        sent.append(copy)

    def shared(slab, part):
        bit = slab & -slab
        send, recv = gather_sems
        remote(
            slabs.at[slab, part], slabs.at[slab, part], send.at[slab, part],
            recv.at[slab, part], "facet", here[bit],
        ).wait_recv()

    def adjoint(slab):
        source = slabs[slab].reshape(2 * SUB, SUB)
        half = jnp.dot(left_table[...], source, preferred_element_type=F32).astype(BF16)
        half = jnp.concatenate([half[:MC], half[MC:]], axis=1)
        window = jnp.dot(half, placed_table[lefts[slab]], preferred_element_type=F32)
        window = window.astype(BF16).reshape(MC // CELLS, CELLS, 2 * cols)
        padded[slab, margin // CELLS : (margin + MC) // CELLS] = window

    share(0, 0, axis_x)
    share(0, 1, axis_y)
    share(0, 0, core)
    share(0, 1, core)
    share(0, 1, axis_x)
    share(0, 0, axis_y)
    adjoint(0)
    shared(1, 0)
    shared(1, 1)
    adjoint(1)
    shared(2, 0)
    share(2, 0, axis_y)
    share(2, 0, core)
    shared(4, 1)
    share(4, 1, axis_x)
    share(4, 1, core)
    shared(2, 1)
    share(2, 1, core)
    shared(4, 0)
    share(4, 0, core)
    adjoint(2)
    adjoint(4)
    shared(3, 0)
    shared(3, 1)
    adjoint(3)
    shared(6, 0)
    share(6, 0, core)
    shared(6, 1)
    share(6, 1, core)
    shared(5, 0)
    shared(5, 1)
    adjoint(5)
    adjoint(6)
    shared(7, 0)
    shared(7, 1)
    adjoint(7)

    piece = rows // pos_v
    spans = row_spans(piece)
    starts = [(margin - top * STEP) // CELLS for top in tops]

    def own_rows(chunk, part):
        at, size = spans[part]
        value = jnp.zeros((size, 2 * cols), F32)
        for slab in range(facets):
            begin = starts[slab] + (chunk * piece + at) // CELLS
            pick = [padded[slab, begin + i] for i in range(size // CELLS)]
            value = value + jnp.concatenate(pick, axis=0).astype(F32)
        return value

    def line_copy(way, chunk, part):
        at, size = spans[part]
        send, recv = line_sems
        return remote(
            staged.at[chunk, pl.ds(at, size)], landed.at[way, chunk, pl.ds(at, size)],
            send.at[way, chunk, part], recv.at[way, chunk, part], "sub", ahead[way],
        )

    def plan(place):
        steps = []
        for way in range(2):
            depth = place if way == 0 else pos_v - 1 - place
            for turn in range(len(spans) * (pos_v - 1 - depth)):
                chunk = turn // len(spans)
                chunk = chunk if way else pos_v - 1 - chunk
                steps.append((turn + depth, depth, way, chunk, turn % len(spans)))
        return sorted(steps)

    for spot in range(pos_v):
        @pl.when(rank == spot)
        def _():
            for _, depth, way, chunk, part in plan(spot):
                at, size = spans[part]
                value = own_rows(chunk, part)
                if depth:
                    line_copy(way, chunk, part).wait_recv()
                    value = value + landed[way, chunk, pl.ds(at, size)].astype(F32)
                staged[chunk, pl.ds(at, size)] = value.astype(BF16)
                line_copy(way, chunk, part).start()
            for part, (at, size) in enumerate(spans):
                value = own_rows(spot, part)
                for way in range(2):
                    if spot != (0, pos_v - 1)[way]:
                        line_copy(way, spot, part).wait_recv()
                        value = value + landed[way, spot, pl.ds(at, size)].astype(F32)
                update[0, 0, pl.ds(at, size)] = value[:, :cols]
                update[0, 1, pl.ds(at, size)] = value[:, cols:]
            for _, depth, way, chunk, part in plan(spot):
                line_copy(way, chunk, part).wait_send()

    for copy in sent:
        copy.wait_send()


def fused(facet_spec, worker, vis_count, bin_offsets, bin_fractions, observed):
    facets = lax.axis_size("facet")
    pos_v = lax.axis_size("sub")
    rows, cols = facet_spec.shape[2:]
    slots = bin_offsets.shape[2]
    block = math.gcd(slots, 2048)
    base, turns = phases(facets)
    piece = rows // pos_v
    parts = len(row_spans(piece))
    dma = pltpu.SemaphoreType.DMA
    pair = lambda *shape: (dma(shape), dma(shape))
    return pl.pallas_call(
        functools.partial(fused_kernel, facets, pos_v, block),
        out_shape=(
            pltpu.VMEM((1, 2, slots), F32),
            pltpu.VMEM((1, 2, piece, cols), F32),
        ),
        in_specs=[VMEM, VMEM, SMEM, SMEM, VMEM, VMEM, VMEM, VMEM],
        out_specs=(VMEM, VMEM),
        scratch_shapes=[
            pltpu.VMEM((2 * MC, 2 * SUB), BF16),
            pltpu.VMEM((2 * SUB, 2 * MC), BF16),
            pltpu.VMEM((pos_v, 2 * SUB, 2 * cols), BF16),
            pltpu.VMEM(((rows - MC) // STEP + 1, 2, cols // STEP, STEP, MC), BF16),
            pltpu.VMEM((facets // 2, 2, SUB, SUB), BF16),
            pltpu.VMEM((facets // 2, 2, SUB, SUB), BF16),
            pltpu.VMEM((3, SUB, SUB), BF16),
            pltpu.VMEM((3, SUB, SUB), BF16),
            pltpu.VMEM((3, SUB, SUB), BF16),
            pltpu.VMEM((3, SUB, SUB), BF16),
            pltpu.VMEM((4, SUB, SUB), F32),
            pltpu.VMEM((2 * SUB, SUB), BF16),
            pltpu.VMEM((SUB, slots), BF16),
            pltpu.VMEM((CELLS, slots), F32),
            pltpu.VMEM((CELLS, slots), jnp.int32),
            pltpu.VMEM((SUB, 2 * SUB), F32),
            pltpu.VMEM((facets, 2, SUB, SUB), BF16),
            pltpu.VMEM((facets, (2 * rows - MC) // CELLS, CELLS, 2 * cols), BF16),
            pltpu.VMEM((pos_v, piece, 2 * cols), BF16),
            pltpu.VMEM((2, pos_v, piece, 2 * cols), BF16),
            pair(facets // 2),
            pair(3),
            pair(3),
            pair(facets, 2),
            pair(2, pos_v, parts),
        ],
        compiler_params=pltpu.CompilerParams(
            collective_id=3, has_side_effects=True, vmem_limit_bytes=56 * 1024 * 1024
        ),
        name="everything",
    )(
        base, turns, worker, vis_count, jnp.swapaxes(facet_spec, 2, 3),
        bin_offsets, bin_fractions, observed,
    )


def on_device(facet_spec, *rest):
    facets = lax.axis_size("facet")
    rows, cols = facet_spec.shape[2:]
    padded_bytes = facets * (2 * rows - MC) * 2 * cols * 2
    fits = len(bits_of(facets)) == 3 and padded_bytes <= 20 * 1024 * 1024
    return (fused if fits else staged_path)(facet_spec, *rest)


def solution(mesh):
    placed = (
        P("facet", None, None, None),
        P(),
        P(("facet", "sub")),
        P(("facet", "sub"), None, None),
        P(("facet", "sub"), None, None),
        P(("facet", "sub"), None, None),
    )
    return jax.shard_map(
        on_device,
        mesh=mesh,
        in_specs=placed,
        out_specs=(P(("facet", "sub"), None, None), P("facet", None, "sub", None)),
        check_vma=False,
    )
```

```python
import functools
import math

import jax
import jax.numpy as jnp
import numpy as np
from jax import lax
from jax.experimental import pallas as pl
from jax.experimental.pallas import tpu as pltpu
from jax.sharding import PartitionSpec as P

SUB = 256
MC = 256
STEP = 64
KS = 8
VB = 512
MESH = pl.DeviceIdType.MESH
VMEM = pl.BlockSpec(memory_space=pltpu.VMEM)
SMEM = pl.BlockSpec(memory_space=pltpu.SMEM)
F32 = jnp.float32
BF16 = jnp.bfloat16


def flip(index, bit):
    return index + bit - 2 * bit * ((index // bit) % 2)


def bits_of(count):
    return [1 << level for level in range(count.bit_length() - 1)]


def routes(count):
    bits = bits_of(count)
    return (bits, bits[:1] + bits[:0:-1])


def greet(count):
    me = lax.axis_index("facet")
    barrier = pltpu.get_barrier_semaphore()
    bits = bits_of(count)
    for bit in bits:
        pl.semaphore_signal(
            barrier, inc=1, device_id={"facet": flip(me, bit)}, device_id_type=MESH
        )
    pl.semaphore_wait(barrier, len(bits))


def remote(src, dst, send, recv, axis, target):
    return pltpu.make_async_remote_copy(
        src_ref=src,
        dst_ref=dst,
        send_sem=send,
        recv_sem=recv,
        device_id={axis: target},
        device_id_type=MESH,
    )


def transform_kernel(
    facets, pos_v, base, turns, worker, spec, slabs, left_adjoint, right_table,
    turned_table, corners, left_table, holder
):
    cols = spec.shape[3]
    pad = (pos_v - 1) * STEP
    me = lax.axis_index("facet")
    rank = lax.axis_index("sub")

    def note(subgrid, carry):
        holder[worker[subgrid]] = subgrid
        return carry

    lax.fori_loop(0, worker.shape[0], note, 0)
    for slab in range(facets):
        member = me
        for bit in bits_of(facets):
            member = flip(member, bit) if slab & bit else member
        subgrid = holder[member * pos_v + rank]
        corners[0, slab] = subgrid // pos_v * STEP
        corners[1, slab] = pad - subgrid % pos_v * STEP

    def turned(facet):
        turn = turns[facet]
        real, imag = turn[0:1], turn[1:2]
        return (base[0] * real - base[1] * imag, base[0] * imag + base[1] * real)

    real, imag = turned(me)
    left_adjoint[:MC, :SUB] = real.astype(BF16)
    left_adjoint[:MC, SUB:] = imag.astype(BF16)
    left_adjoint[MC:, :SUB] = (-imag).astype(BF16)
    left_adjoint[MC:, SUB:] = real.astype(BF16)
    real, imag = real.T, imag.T
    left_table[:SUB, :MC] = real.astype(BF16)
    left_table[:SUB, MC:] = (-imag).astype(BF16)
    left_table[SUB:, :MC] = imag.astype(BF16)
    left_table[SUB:, MC:] = real.astype(BF16)
    real, imag = turned((5 * me + 3) % facets)
    for table, first, second in ((right_table, real, imag), (turned_table, -imag, real)):
        table[:pad] = jnp.zeros((pad, 2 * SUB), BF16)
        table[pad + MC :] = jnp.zeros((pad, 2 * SUB), BF16)
        table[pad : pad + MC, :SUB] = first.astype(BF16)
        table[pad : pad + MC, SUB:] = second.astype(BF16)

    def transform(slab, carry):
        top = pl.multiple_of(corners[0, slab], STEP)
        left = pl.multiple_of(corners[1, slab], STEP)
        window = jnp.concatenate(
            [spec[0, 0, pl.ds(top, MC), :], spec[0, 1, pl.ds(top, MC), :]], axis=0
        )
        table = right_table[pl.ds(left, cols), :]
        mixed = jnp.dot(window, table, preferred_element_type=F32)
        real = mixed[:MC, :SUB] - mixed[MC:, SUB:]
        imag = mixed[:MC, SUB:] + mixed[MC:, :SUB]
        half = jnp.concatenate([real, imag], axis=0).astype(BF16)
        value = jnp.dot(left_table[...], half, preferred_element_type=F32)
        slabs[slab] = value.astype(BF16).reshape(2, SUB, SUB)
        return carry

    lax.fori_loop(0, facets, transform, 0, unroll=2)


def halve_kernel(facets, slabs, grid_out, total, landed, send, recv):
    me = lax.axis_index("facet")
    greet(facets)
    orders = routes(facets)
    levels = len(orders[0])
    sent = []

    def queue(part, level, held):
        rank = lambda slab: tuple(not slab & bit for bit in orders[part][level:])
        return sorted(held, key=rank)

    def copy_of(source, level, slab, part):
        bit = orders[part][level]
        return remote(
            source.at[slab, part], landed.at[level, slab - bit, part],
            send.at[2 * level + part, slab], recv.at[2 * level + part, slab - bit],
            "facet", flip(me, bit),
        )

    def post(source, level, slab, part):
        copy = copy_of(source, level, slab, part)
        copy.start()
        sent.append(copy)

    held = [list(range(facets))] * 2
    pairs = [queue(part, 0, [s for s in held[part] if s & 1]) for part in range(2)]
    for both in zip(*pairs):
        for part, slab in enumerate(both):
            post(slabs, 0, slab, part)
    for level in range(levels):
        held = [[s for s in held[p] if not s & orders[p][level]] for p in range(2)]
        pairs = [queue(part, level + 1, held[part]) for part in range(2)]
        for both in zip(*pairs):
            for part, slab in enumerate(both):
                copy_of(slabs, level, slab + orders[part][level], part).wait_recv()
                source = slabs if level == 0 else total
                value = source[slab, part].astype(F32) + landed[level, slab, part].astype(F32)
                if level == levels - 1:
                    grid_out[part] = value.astype(BF16)
                else:
                    total[slab, part] = value.astype(BF16)
                    if slab & orders[part][level + 1]:
                        post(total, level + 1, slab, part)
    for copy in sent:
        copy.wait_send()


def kernel_columns(offsets, fractions):
    cells = lax.broadcasted_iota(jnp.int32, (SUB, offsets.shape[1]), 0).astype(F32)
    scale = math.sqrt(math.log2(math.e)) * 9.0 / KS
    centred = cells - (offsets.astype(F32) + (0.5 * KS - 0.5))
    distance = centred * scale - (fractions - 0.5) * scale
    inside = jnp.abs(centred) < 0.5 * KS
    return jnp.where(inside, jnp.exp2(-1.0 - distance * distance), 0.0).astype(BF16)


def vis_kernel(count, grid, offsets, fractions, observed, residual, gridded, flipped, total):
    slots = offsets.shape[2]
    live_count = count[0]
    flipped[:SUB] = grid[0].astype(F32).T.astype(BF16)
    flipped[SUB:] = grid[1].astype(F32).T.astype(BF16)
    total[...] = jnp.zeros_like(total)
    residual[...] = jnp.zeros_like(residual)

    def half_block(first):
        span = pl.ds(first, VB)
        u_weights = kernel_columns(offsets[0, 0:1, span], fractions[0, 0:1, span])
        v_weights = kernel_columns(offsets[0, 1:2, span], fractions[0, 1:2, span])
        v_float = v_weights.astype(F32)
        product = jnp.dot(flipped[...], u_weights, preferred_element_type=F32)
        live = first + lax.broadcasted_iota(jnp.int32, (1, VB), 1) < live_count
        weighted = []
        for part in range(2):
            model = jnp.sum(product[part * SUB : (part + 1) * SUB] * v_float, axis=0, keepdims=True)
            row = jnp.where(live, observed[0, part : part + 1, span] - model, 0.0)
            residual[0, part : part + 1, span] = row
            weighted.append((row * v_float).astype(BF16))
        return lax.dot_general(
            u_weights,
            jnp.concatenate(weighted, axis=0),
            (((1,), (1,)), ((), ())),
            preferred_element_type=F32,
        )

    def block(index, carry):
        first = pl.multiple_of(index * 2 * VB, 2 * VB)
        total[...] += half_block(first) + half_block(first + VB)
        return carry

    lax.fori_loop(0, (live_count + 2 * VB - 1) // (2 * VB), block, 0)
    gridded[0] = total[:, :SUB].astype(BF16)
    gridded[1] = total[:, SUB:].astype(BF16)


def gather_kernel(facets, own, slabs, send, recv):
    me = lax.axis_index("facet")
    greet(facets)
    orders = [order[:0:-1] + order[:1] for order in routes(facets)]
    levels = len(orders[0])
    sent = []

    def copy_of(level, slab, part):
        bit = orders[part][level]
        source = slabs.at[slab, part] if slab else own.at[part]
        return remote(
            source, slabs.at[slab + bit, part],
            send.at[part, slab + bit], recv.at[part, slab + bit],
            "facet", flip(me, bit),
        )

    def post(level, slab, part):
        copy = copy_of(level, slab, part)
        copy.start()
        sent.append(copy)

    for level in range(levels):
        for part in range(2):
            post(level, 0, part)
    slabs[0] = own[...]
    held = [[0], [0]]
    for level in range(levels):
        for both in zip(*held):
            for part, slab in enumerate(both):
                copy_of(level, slab, part).wait_recv()
                for later in range(level + 1, levels):
                    post(later, slab + orders[part][level], part)
        held = [held[p] + [s + orders[p][level] for s in held[p]] for p in range(2)]
    for copy in sent:
        copy.wait_send()


def adjoint_kernel(facets, corners, everyone, left_table, right_table, turned_table, pieces, plane):
    cols = plane.shape[1] // 2
    chunk = pieces.shape[1]
    plane[...] = jnp.zeros_like(plane)

    def add_source(slab, carry):
        top = pl.multiple_of(corners[0, slab], STEP)
        left = pl.multiple_of(corners[1, slab], STEP)
        source = everyone[slab].reshape(2 * SUB, SUB)
        half = jnp.dot(left_table[...], source, preferred_element_type=F32)
        row = jnp.concatenate([half[:MC], half[MC:]], axis=1).astype(BF16)
        table = jnp.concatenate(
            [right_table[pl.ds(left, cols), :], turned_table[pl.ds(left, cols), :]], axis=0
        )
        window = lax.dot_general(row, table, (((1,), (1,)), ((), ())), preferred_element_type=F32)
        plane[pl.ds(top, MC), :] += window
        return carry

    lax.fori_loop(0, facets, add_source, 0, unroll=2)
    for piece in range(pieces.shape[0]):
        pieces[piece] = plane[piece * chunk : (piece + 1) * chunk, :].astype(BF16)


def line_kernel(groups, pieces, update, totals, landed, send, recv):
    me = lax.axis_index("sub")
    barrier = pltpu.get_barrier_semaphore()
    inner = (me > 0, me < groups - 1)
    ahead = ((me + 1) % groups, (me + groups - 1) % groups)
    behind = (ahead[1], ahead[0])
    for way in range(2):
        @pl.when(inner[way])
        def _():
            pl.semaphore_signal(
                barrier, inc=1, device_id={"sub": behind[way]}, device_id_type=MESH
            )
    between = jnp.logical_and(inner[0], inner[1])

    @pl.when(between)
    def _():
        pl.semaphore_wait(barrier, 2)

    @pl.when(jnp.logical_not(between))
    def _():
        pl.semaphore_wait(barrier, 1)

    cols = update.shape[3]
    size = pieces.shape[1]
    cut = (size // 2 + 15) // 16 * 16
    spans = (pl.ds(0, cut), pl.ds(cut, size - cut))

    def copy_of(source, way, chunk, part):
        return remote(
            source.at[chunk, spans[part]], landed.at[way, chunk, spans[part]],
            send.at[way, chunk, part], recv.at[way, chunk, part], "sub", ahead[way],
        )

    def plan(place):
        steps = []
        for way in range(2):
            depth = place if way == 0 else groups - 1 - place
            for turn in range(2 * (groups - 1 - depth)):
                chunk = turn // 2 if way else groups - 1 - turn // 2
                steps.append((turn + depth, depth, way, chunk, turn % 2))
        return sorted(steps)

    for place in range(groups):
        @pl.when(me == place)
        def _():
            for _, depth, way, chunk, part in plan(place):
                if depth == 0:
                    copy_of(pieces, way, chunk, part).start()
                    continue
                copy_of(pieces, way, chunk, part).wait_recv()
                totals[way, chunk, spans[part]] = (
                    pieces[chunk, spans[part]].astype(F32)
                    + landed[way, chunk, spans[part]].astype(F32)
                ).astype(BF16)
                copy_of(totals.at[way], way, chunk, part).start()
            for part in range(2):
                span = spans[part]
                value = pieces[place, span].astype(F32)
                for way in range(2):
                    if place != (0, groups - 1)[way]:
                        copy_of(pieces, way, place, part).wait_recv()
                        value = value + landed[way, place, span].astype(F32)
                update[0, 0, span] = value[:, :cols]
                update[0, 1, span] = value[:, cols:]
            for _, depth, way, chunk, part in plan(place):
                copy_of(pieces, way, chunk, part).wait_send()


def phases(facets):
    modulus = SUB * facets
    centred = np.arange(SUB) - SUB // 2
    base = np.exp(2j * np.pi * (np.outer(centred, centred) * facets % modulus) / modulus)
    turn = np.exp(2j * np.pi * (np.outer(np.arange(facets), centred) % modulus) / modulus)
    pair = lambda z: jnp.asarray(np.stack([z.real, z.imag]).astype(np.float32))
    return pair(base * MC ** (-0.5)), jnp.swapaxes(pair(turn), 0, 1)


def staged_path(facet_spec, worker_of_subgrid, vis_count, bin_offsets, bin_fractions, observed):
    facets = lax.axis_size("facet")
    pos_v = lax.axis_size("sub")
    rows = facet_spec.shape[2]
    cols = facet_spec.shape[3]
    pad = (pos_v - 1) * STEP
    slots = bin_offsets.shape[2]
    base, turns = phases(facets)
    levels = len(bits_of(facets))
    slab_shape = (2, SUB, SUB)
    limit = 60 * 1024 * 1024
    slabs, left_adjoint, right, right_turned, corners = pl.pallas_call(
        functools.partial(transform_kernel, facets, pos_v),
        out_shape=(
            jax.ShapeDtypeStruct((facets,) + slab_shape, BF16),
            jax.ShapeDtypeStruct((2 * MC, 2 * SUB), BF16),
            jax.ShapeDtypeStruct((MC + 2 * pad, 2 * SUB), BF16),
            jax.ShapeDtypeStruct((MC + 2 * pad, 2 * SUB), BF16),
            jax.ShapeDtypeStruct((2, facets), jnp.int32),
        ),
        in_specs=[VMEM, VMEM, SMEM, VMEM],
        out_specs=(VMEM, VMEM, VMEM, VMEM, SMEM),
        scratch_shapes=[
            pltpu.VMEM((2 * SUB, 2 * MC), BF16),
            pltpu.SMEM(worker_of_subgrid.shape, jnp.int32),
        ],
        compiler_params=pltpu.CompilerParams(vmem_limit_bytes=limit),
        name="transform",
    )(base, turns, worker_of_subgrid, facet_spec)

    grid = pl.pallas_call(
        functools.partial(halve_kernel, facets),
        out_shape=jax.ShapeDtypeStruct(slab_shape, BF16),
        in_specs=[VMEM],
        out_specs=VMEM,
        scratch_shapes=[
            pltpu.VMEM((facets,) + slab_shape, BF16),
            pltpu.VMEM((levels, facets) + slab_shape, BF16),
            pltpu.SemaphoreType.DMA((2 * levels, facets)),
            pltpu.SemaphoreType.DMA((2 * levels, facets)),
        ],
        compiler_params=pltpu.CompilerParams(
            collective_id=0, has_side_effects=True, vmem_limit_bytes=limit
        ),
        name="sum_grids",
    )(slabs)

    residual, gridded = pl.pallas_call(
        vis_kernel,
        out_shape=(
            jax.ShapeDtypeStruct((1, 2, slots), F32),
            jax.ShapeDtypeStruct(slab_shape, BF16),
        ),
        in_specs=[SMEM, VMEM, VMEM, VMEM, VMEM],
        out_specs=(VMEM, VMEM),
        scratch_shapes=[
            pltpu.VMEM((2 * SUB, SUB), BF16),
            pltpu.VMEM((SUB, 2 * SUB), F32),
        ],
        compiler_params=pltpu.CompilerParams(vmem_limit_bytes=limit),
        name="visibilities",
    )(vis_count, grid, bin_offsets, bin_fractions, observed)

    everyone = pl.pallas_call(
        functools.partial(gather_kernel, facets),
        out_shape=jax.ShapeDtypeStruct((facets,) + slab_shape, BF16),
        in_specs=[VMEM],
        out_specs=VMEM,
        scratch_shapes=[
            pltpu.SemaphoreType.DMA((2, facets)),
            pltpu.SemaphoreType.DMA((2, facets)),
        ],
        compiler_params=pltpu.CompilerParams(
            collective_id=1, has_side_effects=True, vmem_limit_bytes=limit
        ),
        name="gather_grids",
    )(gridded)

    chunk = rows // pos_v
    pieces = pl.pallas_call(
        functools.partial(adjoint_kernel, facets),
        out_shape=jax.ShapeDtypeStruct((pos_v, chunk, 2 * cols), BF16),
        in_specs=[SMEM, VMEM, VMEM, VMEM, VMEM],
        out_specs=VMEM,
        scratch_shapes=[pltpu.VMEM((rows, 2 * cols), F32)],
        compiler_params=pltpu.CompilerParams(vmem_limit_bytes=limit),
        name="adjoint",
    )(corners, everyone, left_adjoint, right, right_turned)

    update = pl.pallas_call(
        functools.partial(line_kernel, pos_v),
        out_shape=jax.ShapeDtypeStruct((1, 2, chunk, cols), F32),
        in_specs=[VMEM],
        out_specs=VMEM,
        scratch_shapes=[
            pltpu.VMEM((2, pos_v, chunk, 2 * cols), BF16),
            pltpu.VMEM((2, pos_v, chunk, 2 * cols), BF16),
            pltpu.SemaphoreType.DMA((2, pos_v, 2)),
            pltpu.SemaphoreType.DMA((2, pos_v, 2)),
        ],
        compiler_params=pltpu.CompilerParams(
            collective_id=2, has_side_effects=True, vmem_limit_bytes=limit
        ),
        name="sum_pieces",
    )(pieces)
    return (residual, update)


CELLS = 16
FILL = 4


def spread(values, groups):
    zero = jnp.zeros_like(values)
    rows = [jnp.where(groups == cell, values, zero) for cell in range(SUB // CELLS)]
    return jnp.concatenate(rows, axis=0)


def compact(offsets, fractions):
    row = lax.broadcasted_iota(jnp.int32, (CELLS, offsets.shape[1]), 0)
    ahead = (row - offsets) & (CELLS - 1)
    scale = math.sqrt(math.log2(math.e)) * 9.0 / KS
    distance = (ahead.astype(F32) - (0.5 * KS - 1.0) - fractions) * scale
    values = jnp.where(ahead < KS, jnp.exp2(-1.0 - distance * distance), 0.0)
    return values.astype(BF16), (offsets + ahead) // CELLS


def gather_cells(product, bits):
    parts = [product[i * CELLS : (i + 1) * CELLS] for i in range(SUB // CELLS)]
    for bit in bits:
        parts = [jnp.where(bit, b, a) for a, b in zip(parts[::2], parts[1::2])]
    return parts[0]


def row_spans(size):
    step = (size // FILL + 15) // 16 * 16
    return [(at, min(step, size - at)) for at in range(0, size, step)]


def fused_kernel(
    facets, pos_v, block, base, turns, worker, count, spec, offsets, fractions, observed,
    residual, update, left_table, right_table, placed_table, views, out_core, in_core,
    out_x, out_y, in_x, in_y, kept, grid, u_dense, v_values, v_groups, total, slabs, padded,
    staged, landed, core_sems, x_sems, y_sems, gather_sems, line_sems
):
    me = lax.axis_index("facet")
    rank = lax.axis_index("sub")
    cols, rows = spec.shape[2], spec.shape[3]
    slots = offsets.shape[2]
    margin = rows - MC
    core, axis_x, axis_y = 1, 2, 4
    here = {bit: flip(me, bit) for bit in (core, axis_x, axis_y)}

    barrier = pltpu.get_barrier_semaphore()
    for bit in here:
        pl.semaphore_signal(barrier, inc=1, device_id={"facet": here[bit]}, device_id_type=MESH)
    inner = (rank > 0, rank < pos_v - 1)
    ahead = ((rank + 1) % pos_v, (rank + pos_v - 1) % pos_v)
    for way in range(2):
        @pl.when(inner[way])
        def _():
            pl.semaphore_signal(
                barrier, inc=1, device_id={"sub": ahead[1 - way]}, device_id_type=MESH
            )

    wanted = []
    for slab in range(facets):
        member = me
        for bit in bits_of(facets):
            member = flip(member, bit) if slab & bit else member
        wanted.append(member * pos_v + rank)

    def note(subgrid, found):
        at = worker[subgrid]
        return tuple(jnp.where(at == w, subgrid, f) for w, f in zip(wanted, found))

    found = lax.fori_loop(
        0, worker.shape[0], note, tuple(jnp.int32(0) for _ in wanted), unroll=8
    )
    tops = [subgrid // pos_v for subgrid in found]
    lefts = [subgrid % pos_v for subgrid in found]

    def turned(facet):
        turn = turns[facet]
        real, imag = turn[0:1], turn[1:2]
        return (base[0] * real - base[1] * imag, base[0] * imag + base[1] * real)

    def quarters(table, real, imag, flipped_first):
        table[:MC, :SUB] = real.astype(BF16)
        table[MC:, SUB:] = real.astype(BF16)
        low, high = (-imag, imag) if flipped_first else (imag, -imag)
        table[:MC, SUB:] = low.astype(BF16)
        table[MC:, :SUB] = high.astype(BF16)

    real, imag = turned(me)
    quarters(left_table, real, imag, False)
    real, imag = turned((5 * me + 3) % facets)
    b_real, b_imag = real.T, imag.T
    quarters(right_table, b_real, b_imag, True)
    for part in range(2):
        even, odd = spec[0, part], spec[0, part, :, STEP:]
        for top in range(views.shape[0]):
            at = top // 2 * 2 * STEP
            view = (odd if top % 2 else even)[:, at : at + MC]
            views[top, part] = view.reshape(cols // STEP, STEP, MC)

    @pl.when(jnp.logical_and(inner[0], inner[1]))
    def _():
        pl.semaphore_wait(barrier, 5)

    @pl.when(jnp.logical_not(jnp.logical_and(inner[0], inner[1])))
    def _():
        pl.semaphore_wait(barrier, 4)

    sent = []

    def post(source, target, sems, index, bit):
        send, recv = sems
        copy = remote(source, target, send.at[index], recv.at[index], "facet", here[bit])
        copy.start()
        sent.append(copy)

    def arrive(source, target, sems, index, bit):
        send, recv = sems
        remote(source, target, send.at[index], recv.at[index], "facet", here[bit]).wait_recv()

    def contribution(slab):
        top, left = tops[slab], lefts[slab]
        window = jnp.concatenate(
            [
                jnp.concatenate([views[top, part, left + i] for i in range(MC // STEP)], axis=0)
                for part in range(2)
            ],
            axis=1,
        )
        half = jnp.dot(window, left_table[...], preferred_element_type=F32).astype(BF16)
        half = jnp.concatenate([half[:, :SUB], half[:, SUB:]], axis=0)
        return jnp.dot(right_table[...], half, preferred_element_type=F32)

    def to_partner(slab):
        value = contribution(slab)
        out_core[slab // 2] = value.astype(BF16).reshape(2, SUB, SUB)
        post(out_core.at[slab // 2], in_core.at[slab // 2], core_sems, slab // 2, core)

    def own(slab):
        value = contribution(slab).reshape(2, SUB, SUB)
        arrive(out_core.at[slab // 2], in_core.at[slab // 2], core_sems, slab // 2, core)
        return value + in_core[slab // 2].astype(F32)

    half_rows = SUB // 2
    halves = (slice(0, half_rows), slice(half_rows, SUB))
    lanes = {axis_x: (out_x, in_x, x_sems), axis_y: (out_y, in_y, y_sems)}

    def hold(bit, part, index, value):
        lanes[bit][0][part, index] = value.astype(BF16)

    def go(bit, part, index):
        out, landing, sems = lanes[bit]
        post(out.at[part, index], landing.at[part, index], sems, (part, index), bit)

    def come(bit, part, index):
        out, landing, sems = lanes[bit]
        arrive(out.at[part, index], landing.at[part, index], sems, (part, index), bit)
        return landing[part, index].astype(F32)

    to_partner(7)
    to_partner(3)
    to_partner(5)
    value = own(6)
    for part in range(2):
        for bit, half in ((axis_x, 0), (axis_y, 1)):
            hold(bit, part, 0, value[part, halves[half]])
            if part == 0:
                go(bit, 0, 0)
    for slab, bit, near, far, keep in ((2, axis_x, 0, 1, 0), (4, axis_y, 1, 0, 1)):
        value = own(slab)
        for part in range(2):
            hold(bit, part, 1, value[part, halves[near]])
            if part == 0:
                go(bit, 0, 1)
                go(bit, 1, 0)
            kept[keep, part] = value[part, halves[far]]
    to_partner(1)
    value = own(0)
    for part in range(2):
        for half in range(2):
            kept[2 + half, part] = value[part, halves[half]]

    def turn_corner(part):
        for bit, other, keep in ((axis_x, axis_y, 0), (axis_y, axis_x, 1)):
            hold(bit, part, 2, kept[keep, part] + come(other, part, 0))
            go(bit, part, 2)

    turn_corner(0)
    go(axis_x, 1, 1)
    go(axis_y, 1, 1)

    def place(table, first, second):
        blank = jnp.zeros((SUB, cols * 2 - MC), F32)
        first = jnp.concatenate([first, blank], axis=1)
        second = pltpu.roll(jnp.concatenate([second, blank], axis=1), cols, 1)
        value = first + second
        for left in range(pos_v):
            moved = pltpu.roll(value, left * STEP, 1) if left else value
            placed_table[left, table * SUB : (table + 1) * SUB] = moved.astype(BF16)

    place(0, b_real, -b_imag)
    place(1, b_imag, b_real)
    turn_corner(1)

    def prepare(index, carry):
        span = pl.ds(pl.multiple_of(index * block, block), block)
        values, groups = compact(offsets[0, 0:1, span], fractions[0, 0:1, span])
        u_dense[:, span] = spread(values, groups.astype(jnp.int16))
        values, groups = compact(offsets[0, 1:2, span], fractions[0, 1:2, span])
        v_values[:, span] = values.astype(F32)
        v_groups[:, span] = groups
        return carry

    lax.fori_loop(0, slots // block, prepare, 0, unroll=2)

    def clear(slab, carry):
        blank = jnp.zeros((margin // CELLS, CELLS, 2 * cols), BF16)
        padded[slab, : margin // CELLS] = blank
        padded[slab, (margin + MC) // CELLS :] = blank
        return carry

    total[...] = jnp.zeros_like(total)
    live_count = count[0]

    def visit(part, index, carry):
        first = pl.multiple_of(index * block, block)
        span = pl.ds(first, block)
        u_weights = u_dense[:, span]
        values, groups = v_values[:, span], v_groups[:, span]
        product = jnp.dot(grid[part], u_weights, preferred_element_type=F32)
        bits = [(groups & bit) != 0 for bit in bits_of(SUB // CELLS)]
        live = first + lax.broadcasted_iota(jnp.int32, (1, block), 1) < live_count
        model = jnp.sum(gather_cells(product, bits) * values, axis=0, keepdims=True)
        row = jnp.where(live, observed[0, part : part + 1, span] - model, 0.0)
        residual[0, part : part + 1, span] = row
        total[part] += lax.dot_general(
            u_weights,
            spread((row * values).astype(BF16), groups.astype(jnp.int16)),
            (((1,), (1,)), ((), ())),
            preferred_element_type=F32,
        )
        return carry

    def visibilities(part):
        for bit, other, half in ((axis_x, axis_y, 0), (axis_y, axis_x, 1)):
            value = kept[2 + half, part] + come(bit, part, 1) + come(other, part, 2)
            grid[part, halves[half]] = value.astype(BF16)
        lax.fori_loop(0, slots // block, functools.partial(visit, part), 0, unroll=True)
        slabs[0, part] = total[part].astype(BF16)

    def gathered(slab, part, bit, half):
        send, recv = gather_sems
        index = (slab + bit, part, half or 0)
        rows_of = slice(None) if half is None else halves[half]
        return remote(
            slabs.at[slab, part, rows_of], slabs.at[slab + bit, part, rows_of],
            send.at[index], recv.at[index], "facet", here[bit],
        )

    def share(slab, part, bit, half=None):
        copy = gathered(slab, part, bit, half)
        copy.start()
        sent.append(copy)

    def shared(slab, part, half=None):
        bit = slab & -slab
        gathered(slab - bit, part, bit, half).wait_recv()

    def adjoint(slab):
        source = slabs[slab].reshape(2 * SUB, SUB)
        half = jnp.dot(left_table[...], source, preferred_element_type=F32).astype(BF16)
        half = jnp.concatenate([half[:MC], half[MC:]], axis=1)
        window = jnp.dot(half, placed_table[lefts[slab]], preferred_element_type=F32)
        window = window.astype(BF16).reshape(MC // CELLS, CELLS, 2 * cols)
        padded[slab, margin // CELLS : (margin + MC) // CELLS] = window

    for part in range(2):
        visibilities(part)
        for bit in (axis_x, axis_y, core):
            share(0, part, bit)

    def pass_on(part):
        for slab, bit, half in ((axis_x, axis_y, 0), (axis_y, axis_x, 1)):
            shared(slab, part)
            share(slab, part, bit, half)
            share(slab, part, core)

    def pass_far(part):
        for half in range(2):
            bit = (axis_y, axis_x)[half]
            gathered(6 - bit, part, bit, half).wait_recv()
            share(6, part, core, half)

    def complete(slab):
        for part in range(2):
            if slab == 7:
                for half in range(2):
                    shared(slab, part, half)
            else:
                shared(slab, part)
        adjoint(slab)

    adjoint(0)
    pass_on(0)
    complete(1)
    lax.fori_loop(0, facets, clear, 0)
    pass_on(1)
    adjoint(2)
    adjoint(4)
    pass_far(0)
    complete(3)
    pass_far(1)
    complete(5)
    adjoint(6)
    complete(7)

    piece = rows // pos_v
    spans = row_spans(piece)
    starts = [(margin - top * STEP) // CELLS for top in tops]

    def own_rows(chunk, part):
        at, size = spans[part]
        value = jnp.zeros((size, 2 * cols), F32)
        for slab in range(facets):
            begin = starts[slab] + (chunk * piece + at) // CELLS
            pick = [padded[slab, begin + i] for i in range(size // CELLS)]
            value = value + jnp.concatenate(pick, axis=0).astype(F32)
        return value

    def line_copy(way, chunk, part):
        at, size = spans[part]
        send, recv = line_sems
        return remote(
            staged.at[chunk, pl.ds(at, size)], landed.at[way, chunk, pl.ds(at, size)],
            send.at[way, chunk, part], recv.at[way, chunk, part], "sub", ahead[way],
        )

    def plan(place):
        steps = []
        for way in range(2):
            depth = place if way == 0 else pos_v - 1 - place
            for turn in range(len(spans) * (pos_v - 1 - depth)):
                chunk = turn // len(spans)
                chunk = chunk if way else pos_v - 1 - chunk
                steps.append((turn + depth, depth, way, chunk, turn % len(spans)))
        return sorted(steps)

    for spot in range(pos_v):
        @pl.when(rank == spot)
        def _():
            for _, depth, way, chunk, part in plan(spot):
                at, size = spans[part]
                value = own_rows(chunk, part)
                if depth:
                    line_copy(way, chunk, part).wait_recv()
                    value = value + landed[way, chunk, pl.ds(at, size)].astype(F32)
                staged[chunk, pl.ds(at, size)] = value.astype(BF16)
                line_copy(way, chunk, part).start()
            for part, (at, size) in enumerate(spans):
                value = own_rows(spot, part)
                for way in range(2):
                    if spot != (0, pos_v - 1)[way]:
                        line_copy(way, spot, part).wait_recv()
                        value = value + landed[way, spot, pl.ds(at, size)].astype(F32)
                update[0, 0, pl.ds(at, size)] = value[:, :cols]
                update[0, 1, pl.ds(at, size)] = value[:, cols:]
            for _, depth, way, chunk, part in plan(spot):
                line_copy(way, chunk, part).wait_send()

    for copy in sent:
        copy.wait_send()


def fused(facet_spec, worker, vis_count, bin_offsets, bin_fractions, observed):
    facets = lax.axis_size("facet")
    pos_v = lax.axis_size("sub")
    rows, cols = facet_spec.shape[2:]
    slots = bin_offsets.shape[2]
    block = math.gcd(slots, 2048)
    base, turns = phases(facets)
    piece = rows // pos_v
    parts = len(row_spans(piece))
    dma = pltpu.SemaphoreType.DMA
    pair = lambda *shape: (dma(shape), dma(shape))
    return pl.pallas_call(
        functools.partial(fused_kernel, facets, pos_v, block),
        out_shape=(
            pltpu.VMEM((1, 2, slots), F32),
            pltpu.VMEM((1, 2, piece, cols), F32),
        ),
        in_specs=[VMEM, VMEM, SMEM, SMEM, VMEM, VMEM, VMEM, VMEM],
        out_specs=(VMEM, VMEM),
        scratch_shapes=[
            pltpu.VMEM((2 * MC, 2 * SUB), BF16),
            pltpu.VMEM((2 * SUB, 2 * MC), BF16),
            pltpu.VMEM((pos_v, 2 * SUB, 2 * cols), BF16),
            pltpu.VMEM(((rows - MC) // STEP + 1, 2, cols // STEP, STEP, MC), BF16),
            pltpu.VMEM((facets // 2, 2, SUB, SUB), BF16),
            pltpu.VMEM((facets // 2, 2, SUB, SUB), BF16),
            pltpu.VMEM((2, 3, SUB // 2, SUB), BF16),
            pltpu.VMEM((2, 3, SUB // 2, SUB), BF16),
            pltpu.VMEM((2, 3, SUB // 2, SUB), BF16),
            pltpu.VMEM((2, 3, SUB // 2, SUB), BF16),
            pltpu.VMEM((4, 2, SUB // 2, SUB), F32),
            pltpu.VMEM((2, SUB, SUB), BF16),
            pltpu.VMEM((SUB, slots), BF16),
            pltpu.VMEM((CELLS, slots), F32),
            pltpu.VMEM((CELLS, slots), jnp.int32),
            pltpu.VMEM((2, SUB, SUB), F32),
            pltpu.VMEM((facets, 2, SUB, SUB), BF16),
            pltpu.VMEM((facets, (2 * rows - MC) // CELLS, CELLS, 2 * cols), BF16),
            pltpu.VMEM((pos_v, piece, 2 * cols), BF16),
            pltpu.VMEM((2, pos_v, piece, 2 * cols), BF16),
            pair(facets // 2),
            pair(2, 3),
            pair(2, 3),
            pair(facets, 2, 2),
            pair(2, pos_v, parts),
        ],
        compiler_params=pltpu.CompilerParams(
            collective_id=3, has_side_effects=True, vmem_limit_bytes=56 * 1024 * 1024
        ),
        name="everything",
    )(
        base, turns, worker, vis_count, jnp.swapaxes(facet_spec, 2, 3),
        bin_offsets, bin_fractions, observed,
    )


def on_device(facet_spec, *rest):
    facets = lax.axis_size("facet")
    rows, cols = facet_spec.shape[2:]
    padded_bytes = facets * (2 * rows - MC) * 2 * cols * 2
    fits = len(bits_of(facets)) == 3 and padded_bytes <= 20 * 1024 * 1024
    return (fused if fits else staged_path)(facet_spec, *rest)


def solution(mesh):
    placed = (
        P("facet", None, None, None),
        P(),
        P(("facet", "sub")),
        P(("facet", "sub"), None, None),
        P(("facet", "sub"), None, None),
        P(("facet", "sub"), None, None),
    )
    return jax.shard_map(
        on_device,
        mesh=mesh,
        in_specs=placed,
        out_specs=(P(("facet", "sub"), None, None), P("facet", None, "sub", None)),
        check_vma=False,
    )
```

```python
import functools
import math

import jax
import jax.numpy as jnp
import numpy as np
from jax import lax
from jax.experimental import pallas as pl
from jax.experimental.pallas import tpu as pltpu
from jax.sharding import PartitionSpec as P

SUB = 256
MC = 256
STEP = 64
KS = 8
VB = 512
MESH = pl.DeviceIdType.MESH
VMEM = pl.BlockSpec(memory_space=pltpu.VMEM)
SMEM = pl.BlockSpec(memory_space=pltpu.SMEM)
F32 = jnp.float32
BF16 = jnp.bfloat16


def flip(index, bit):
    return index + bit - 2 * bit * ((index // bit) % 2)


def bits_of(count):
    return [1 << level for level in range(count.bit_length() - 1)]


def routes(count):
    bits = bits_of(count)
    return (bits, bits[:1] + bits[:0:-1])


def greet(count):
    me = lax.axis_index("facet")
    barrier = pltpu.get_barrier_semaphore()
    bits = bits_of(count)
    for bit in bits:
        pl.semaphore_signal(
            barrier, inc=1, device_id={"facet": flip(me, bit)}, device_id_type=MESH
        )
    pl.semaphore_wait(barrier, len(bits))


def remote(src, dst, send, recv, axis, target):
    return pltpu.make_async_remote_copy(
        src_ref=src,
        dst_ref=dst,
        send_sem=send,
        recv_sem=recv,
        device_id={axis: target},
        device_id_type=MESH,
    )


def transform_kernel(
    facets, pos_v, base, turns, worker, spec, slabs, left_adjoint, right_table,
    turned_table, corners, left_table, holder
):
    cols = spec.shape[3]
    pad = (pos_v - 1) * STEP
    me = lax.axis_index("facet")
    rank = lax.axis_index("sub")

    def note(subgrid, carry):
        holder[worker[subgrid]] = subgrid
        return carry

    lax.fori_loop(0, worker.shape[0], note, 0)
    for slab in range(facets):
        member = me
        for bit in bits_of(facets):
            member = flip(member, bit) if slab & bit else member
        subgrid = holder[member * pos_v + rank]
        corners[0, slab] = subgrid // pos_v * STEP
        corners[1, slab] = pad - subgrid % pos_v * STEP

    def turned(facet):
        turn = turns[facet]
        real, imag = turn[0:1], turn[1:2]
        return (base[0] * real - base[1] * imag, base[0] * imag + base[1] * real)

    real, imag = turned(me)
    left_adjoint[:MC, :SUB] = real.astype(BF16)
    left_adjoint[:MC, SUB:] = imag.astype(BF16)
    left_adjoint[MC:, :SUB] = (-imag).astype(BF16)
    left_adjoint[MC:, SUB:] = real.astype(BF16)
    real, imag = real.T, imag.T
    left_table[:SUB, :MC] = real.astype(BF16)
    left_table[:SUB, MC:] = (-imag).astype(BF16)
    left_table[SUB:, :MC] = imag.astype(BF16)
    left_table[SUB:, MC:] = real.astype(BF16)
    real, imag = turned((5 * me + 3) % facets)
    for table, first, second in ((right_table, real, imag), (turned_table, -imag, real)):
        table[:pad] = jnp.zeros((pad, 2 * SUB), BF16)
        table[pad + MC :] = jnp.zeros((pad, 2 * SUB), BF16)
        table[pad : pad + MC, :SUB] = first.astype(BF16)
        table[pad : pad + MC, SUB:] = second.astype(BF16)

    def transform(slab, carry):
        top = pl.multiple_of(corners[0, slab], STEP)
        left = pl.multiple_of(corners[1, slab], STEP)
        window = jnp.concatenate(
            [spec[0, 0, pl.ds(top, MC), :], spec[0, 1, pl.ds(top, MC), :]], axis=0
        )
        table = right_table[pl.ds(left, cols), :]
        mixed = jnp.dot(window, table, preferred_element_type=F32)
        real = mixed[:MC, :SUB] - mixed[MC:, SUB:]
        imag = mixed[:MC, SUB:] + mixed[MC:, :SUB]
        half = jnp.concatenate([real, imag], axis=0).astype(BF16)
        value = jnp.dot(left_table[...], half, preferred_element_type=F32)
        slabs[slab] = value.astype(BF16).reshape(2, SUB, SUB)
        return carry

    lax.fori_loop(0, facets, transform, 0, unroll=2)


def halve_kernel(facets, slabs, grid_out, total, landed, send, recv):
    me = lax.axis_index("facet")
    greet(facets)
    orders = routes(facets)
    levels = len(orders[0])
    sent = []

    def queue(part, level, held):
        rank = lambda slab: tuple(not slab & bit for bit in orders[part][level:])
        return sorted(held, key=rank)

    def copy_of(source, level, slab, part):
        bit = orders[part][level]
        return remote(
            source.at[slab, part], landed.at[level, slab - bit, part],
            send.at[2 * level + part, slab], recv.at[2 * level + part, slab - bit],
            "facet", flip(me, bit),
        )

    def post(source, level, slab, part):
        copy = copy_of(source, level, slab, part)
        copy.start()
        sent.append(copy)

    held = [list(range(facets))] * 2
    pairs = [queue(part, 0, [s for s in held[part] if s & 1]) for part in range(2)]
    for both in zip(*pairs):
        for part, slab in enumerate(both):
            post(slabs, 0, slab, part)
    for level in range(levels):
        held = [[s for s in held[p] if not s & orders[p][level]] for p in range(2)]
        pairs = [queue(part, level + 1, held[part]) for part in range(2)]
        for both in zip(*pairs):
            for part, slab in enumerate(both):
                copy_of(slabs, level, slab + orders[part][level], part).wait_recv()
                source = slabs if level == 0 else total
                value = source[slab, part].astype(F32) + landed[level, slab, part].astype(F32)
                if level == levels - 1:
                    grid_out[part] = value.astype(BF16)
                else:
                    total[slab, part] = value.astype(BF16)
                    if slab & orders[part][level + 1]:
                        post(total, level + 1, slab, part)
    for copy in sent:
        copy.wait_send()


def kernel_columns(offsets, fractions):
    cells = lax.broadcasted_iota(jnp.int32, (SUB, offsets.shape[1]), 0).astype(F32)
    scale = math.sqrt(math.log2(math.e)) * 9.0 / KS
    centred = cells - (offsets.astype(F32) + (0.5 * KS - 0.5))
    distance = centred * scale - (fractions - 0.5) * scale
    inside = jnp.abs(centred) < 0.5 * KS
    return jnp.where(inside, jnp.exp2(-1.0 - distance * distance), 0.0).astype(BF16)


def vis_kernel(count, grid, offsets, fractions, observed, residual, gridded, flipped, total):
    slots = offsets.shape[2]
    live_count = count[0]
    flipped[:SUB] = grid[0].astype(F32).T.astype(BF16)
    flipped[SUB:] = grid[1].astype(F32).T.astype(BF16)
    total[...] = jnp.zeros_like(total)
    residual[...] = jnp.zeros_like(residual)

    def half_block(first):
        span = pl.ds(first, VB)
        u_weights = kernel_columns(offsets[0, 0:1, span], fractions[0, 0:1, span])
        v_weights = kernel_columns(offsets[0, 1:2, span], fractions[0, 1:2, span])
        v_float = v_weights.astype(F32)
        product = jnp.dot(flipped[...], u_weights, preferred_element_type=F32)
        live = first + lax.broadcasted_iota(jnp.int32, (1, VB), 1) < live_count
        weighted = []
        for part in range(2):
            model = jnp.sum(product[part * SUB : (part + 1) * SUB] * v_float, axis=0, keepdims=True)
            row = jnp.where(live, observed[0, part : part + 1, span] - model, 0.0)
            residual[0, part : part + 1, span] = row
            weighted.append((row * v_float).astype(BF16))
        return lax.dot_general(
            u_weights,
            jnp.concatenate(weighted, axis=0),
            (((1,), (1,)), ((), ())),
            preferred_element_type=F32,
        )

    def block(index, carry):
        first = pl.multiple_of(index * 2 * VB, 2 * VB)
        total[...] += half_block(first) + half_block(first + VB)
        return carry

    lax.fori_loop(0, (live_count + 2 * VB - 1) // (2 * VB), block, 0)
    gridded[0] = total[:, :SUB].astype(BF16)
    gridded[1] = total[:, SUB:].astype(BF16)


def gather_kernel(facets, own, slabs, send, recv):
    me = lax.axis_index("facet")
    greet(facets)
    orders = [order[:0:-1] + order[:1] for order in routes(facets)]
    levels = len(orders[0])
    sent = []

    def copy_of(level, slab, part):
        bit = orders[part][level]
        source = slabs.at[slab, part] if slab else own.at[part]
        return remote(
            source, slabs.at[slab + bit, part],
            send.at[part, slab + bit], recv.at[part, slab + bit],
            "facet", flip(me, bit),
        )

    def post(level, slab, part):
        copy = copy_of(level, slab, part)
        copy.start()
        sent.append(copy)

    for level in range(levels):
        for part in range(2):
            post(level, 0, part)
    slabs[0] = own[...]
    held = [[0], [0]]
    for level in range(levels):
        for both in zip(*held):
            for part, slab in enumerate(both):
                copy_of(level, slab, part).wait_recv()
                for later in range(level + 1, levels):
                    post(later, slab + orders[part][level], part)
        held = [held[p] + [s + orders[p][level] for s in held[p]] for p in range(2)]
    for copy in sent:
        copy.wait_send()


def adjoint_kernel(facets, corners, everyone, left_table, right_table, turned_table, pieces, plane):
    cols = plane.shape[1] // 2
    chunk = pieces.shape[1]
    plane[...] = jnp.zeros_like(plane)

    def add_source(slab, carry):
        top = pl.multiple_of(corners[0, slab], STEP)
        left = pl.multiple_of(corners[1, slab], STEP)
        source = everyone[slab].reshape(2 * SUB, SUB)
        half = jnp.dot(left_table[...], source, preferred_element_type=F32)
        row = jnp.concatenate([half[:MC], half[MC:]], axis=1).astype(BF16)
        table = jnp.concatenate(
            [right_table[pl.ds(left, cols), :], turned_table[pl.ds(left, cols), :]], axis=0
        )
        window = lax.dot_general(row, table, (((1,), (1,)), ((), ())), preferred_element_type=F32)
        plane[pl.ds(top, MC), :] += window
        return carry

    lax.fori_loop(0, facets, add_source, 0, unroll=2)
    for piece in range(pieces.shape[0]):
        pieces[piece] = plane[piece * chunk : (piece + 1) * chunk, :].astype(BF16)


def line_kernel(groups, pieces, update, totals, landed, send, recv):
    me = lax.axis_index("sub")
    barrier = pltpu.get_barrier_semaphore()
    inner = (me > 0, me < groups - 1)
    ahead = ((me + 1) % groups, (me + groups - 1) % groups)
    behind = (ahead[1], ahead[0])
    for way in range(2):
        @pl.when(inner[way])
        def _():
            pl.semaphore_signal(
                barrier, inc=1, device_id={"sub": behind[way]}, device_id_type=MESH
            )
    between = jnp.logical_and(inner[0], inner[1])

    @pl.when(between)
    def _():
        pl.semaphore_wait(barrier, 2)

    @pl.when(jnp.logical_not(between))
    def _():
        pl.semaphore_wait(barrier, 1)

    cols = update.shape[3]
    size = pieces.shape[1]
    cut = (size // 2 + 15) // 16 * 16
    spans = (pl.ds(0, cut), pl.ds(cut, size - cut))

    def copy_of(source, way, chunk, part):
        return remote(
            source.at[chunk, spans[part]], landed.at[way, chunk, spans[part]],
            send.at[way, chunk, part], recv.at[way, chunk, part], "sub", ahead[way],
        )

    def plan(place):
        steps = []
        for way in range(2):
            depth = place if way == 0 else groups - 1 - place
            for turn in range(2 * (groups - 1 - depth)):
                chunk = turn // 2 if way else groups - 1 - turn // 2
                steps.append((turn + depth, depth, way, chunk, turn % 2))
        return sorted(steps)

    for place in range(groups):
        @pl.when(me == place)
        def _():
            for _, depth, way, chunk, part in plan(place):
                if depth == 0:
                    copy_of(pieces, way, chunk, part).start()
                    continue
                copy_of(pieces, way, chunk, part).wait_recv()
                totals[way, chunk, spans[part]] = (
                    pieces[chunk, spans[part]].astype(F32)
                    + landed[way, chunk, spans[part]].astype(F32)
                ).astype(BF16)
                copy_of(totals.at[way], way, chunk, part).start()
            for part in range(2):
                span = spans[part]
                value = pieces[place, span].astype(F32)
                for way in range(2):
                    if place != (0, groups - 1)[way]:
                        copy_of(pieces, way, place, part).wait_recv()
                        value = value + landed[way, place, span].astype(F32)
                update[0, 0, span] = value[:, :cols]
                update[0, 1, span] = value[:, cols:]
            for _, depth, way, chunk, part in plan(place):
                copy_of(pieces, way, chunk, part).wait_send()


def phases(facets):
    modulus = SUB * facets
    centred = np.arange(SUB) - SUB // 2
    base = np.exp(2j * np.pi * (np.outer(centred, centred) * facets % modulus) / modulus)
    turn = np.exp(2j * np.pi * (np.outer(np.arange(facets), centred) % modulus) / modulus)
    pair = lambda z: jnp.asarray(np.stack([z.real, z.imag]).astype(np.float32))
    return pair(base * MC ** (-0.5)), jnp.swapaxes(pair(turn), 0, 1)


def staged_path(facet_spec, worker_of_subgrid, vis_count, bin_offsets, bin_fractions, observed):
    facets = lax.axis_size("facet")
    pos_v = lax.axis_size("sub")
    rows = facet_spec.shape[2]
    cols = facet_spec.shape[3]
    pad = (pos_v - 1) * STEP
    slots = bin_offsets.shape[2]
    base, turns = phases(facets)
    levels = len(bits_of(facets))
    slab_shape = (2, SUB, SUB)
    limit = 60 * 1024 * 1024
    slabs, left_adjoint, right, right_turned, corners = pl.pallas_call(
        functools.partial(transform_kernel, facets, pos_v),
        out_shape=(
            jax.ShapeDtypeStruct((facets,) + slab_shape, BF16),
            jax.ShapeDtypeStruct((2 * MC, 2 * SUB), BF16),
            jax.ShapeDtypeStruct((MC + 2 * pad, 2 * SUB), BF16),
            jax.ShapeDtypeStruct((MC + 2 * pad, 2 * SUB), BF16),
            jax.ShapeDtypeStruct((2, facets), jnp.int32),
        ),
        in_specs=[VMEM, VMEM, SMEM, VMEM],
        out_specs=(VMEM, VMEM, VMEM, VMEM, SMEM),
        scratch_shapes=[
            pltpu.VMEM((2 * SUB, 2 * MC), BF16),
            pltpu.SMEM(worker_of_subgrid.shape, jnp.int32),
        ],
        compiler_params=pltpu.CompilerParams(vmem_limit_bytes=limit),
        name="transform",
    )(base, turns, worker_of_subgrid, facet_spec)

    grid = pl.pallas_call(
        functools.partial(halve_kernel, facets),
        out_shape=jax.ShapeDtypeStruct(slab_shape, BF16),
        in_specs=[VMEM],
        out_specs=VMEM,
        scratch_shapes=[
            pltpu.VMEM((facets,) + slab_shape, BF16),
            pltpu.VMEM((levels, facets) + slab_shape, BF16),
            pltpu.SemaphoreType.DMA((2 * levels, facets)),
            pltpu.SemaphoreType.DMA((2 * levels, facets)),
        ],
        compiler_params=pltpu.CompilerParams(
            collective_id=0, has_side_effects=True, vmem_limit_bytes=limit
        ),
        name="sum_grids",
    )(slabs)

    residual, gridded = pl.pallas_call(
        vis_kernel,
        out_shape=(
            jax.ShapeDtypeStruct((1, 2, slots), F32),
            jax.ShapeDtypeStruct(slab_shape, BF16),
        ),
        in_specs=[SMEM, VMEM, VMEM, VMEM, VMEM],
        out_specs=(VMEM, VMEM),
        scratch_shapes=[
            pltpu.VMEM((2 * SUB, SUB), BF16),
            pltpu.VMEM((SUB, 2 * SUB), F32),
        ],
        compiler_params=pltpu.CompilerParams(vmem_limit_bytes=limit),
        name="visibilities",
    )(vis_count, grid, bin_offsets, bin_fractions, observed)

    everyone = pl.pallas_call(
        functools.partial(gather_kernel, facets),
        out_shape=jax.ShapeDtypeStruct((facets,) + slab_shape, BF16),
        in_specs=[VMEM],
        out_specs=VMEM,
        scratch_shapes=[
            pltpu.SemaphoreType.DMA((2, facets)),
            pltpu.SemaphoreType.DMA((2, facets)),
        ],
        compiler_params=pltpu.CompilerParams(
            collective_id=1, has_side_effects=True, vmem_limit_bytes=limit
        ),
        name="gather_grids",
    )(gridded)

    chunk = rows // pos_v
    pieces = pl.pallas_call(
        functools.partial(adjoint_kernel, facets),
        out_shape=jax.ShapeDtypeStruct((pos_v, chunk, 2 * cols), BF16),
        in_specs=[SMEM, VMEM, VMEM, VMEM, VMEM],
        out_specs=VMEM,
        scratch_shapes=[pltpu.VMEM((rows, 2 * cols), F32)],
        compiler_params=pltpu.CompilerParams(vmem_limit_bytes=limit),
        name="adjoint",
    )(corners, everyone, left_adjoint, right, right_turned)

    update = pl.pallas_call(
        functools.partial(line_kernel, pos_v),
        out_shape=jax.ShapeDtypeStruct((1, 2, chunk, cols), F32),
        in_specs=[VMEM],
        out_specs=VMEM,
        scratch_shapes=[
            pltpu.VMEM((2, pos_v, chunk, 2 * cols), BF16),
            pltpu.VMEM((2, pos_v, chunk, 2 * cols), BF16),
            pltpu.SemaphoreType.DMA((2, pos_v, 2)),
            pltpu.SemaphoreType.DMA((2, pos_v, 2)),
        ],
        compiler_params=pltpu.CompilerParams(
            collective_id=2, has_side_effects=True, vmem_limit_bytes=limit
        ),
        name="sum_pieces",
    )(pieces)
    return (residual, update)


CELLS = 16
FILL = 3


def spread(values, groups):
    zero = jnp.zeros_like(values)
    rows = [jnp.where(groups == cell, values, zero) for cell in range(SUB // CELLS)]
    return jnp.concatenate(rows, axis=0)


def compact(offsets, fractions):
    row = lax.broadcasted_iota(jnp.int32, (CELLS, offsets.shape[1]), 0)
    ahead = (row - offsets) & (CELLS - 1)
    scale = math.sqrt(math.log2(math.e)) * 9.0 / KS
    distance = (ahead.astype(F32) - (0.5 * KS - 1.0) - fractions) * scale
    values = jnp.where(ahead < KS, jnp.exp2(-1.0 - distance * distance), 0.0)
    return values.astype(BF16), (offsets + ahead) // CELLS


def gather_cells(product, bits):
    parts = [product[i * CELLS : (i + 1) * CELLS] for i in range(SUB // CELLS)]
    for bit in bits:
        parts = [jnp.where(bit, b, a) for a, b in zip(parts[::2], parts[1::2])]
    return parts[0]


def row_spans(size):
    step = (size // FILL + 15) // 16 * 16
    return [(at, min(step, size - at)) for at in range(0, size, step)]


def fused_kernel(
    facets, pos_v, block, base, turns, worker, count, spec, offsets, fractions, observed,
    residual, update, left_table, right_table, placed_table, views, out_core, in_core,
    out_x, out_y, in_x, in_y, kept, grid, u_dense, v_values, v_groups, total, slabs, padded,
    staged, landed, guest_slabs, lone, extra, core_sems, x_sems, y_sems, gather_sems,
    line_sems, guest_sems, hand_sems
):
    me = lax.axis_index("facet")
    rank = lax.axis_index("sub")
    cols, rows = spec.shape[2], spec.shape[3]
    slots = offsets.shape[2]
    margin = rows - MC
    core, axis_x, axis_y = 1, 2, 4
    here = {bit: flip(me, bit) for bit in (core, axis_x, axis_y)}

    barrier = pltpu.get_barrier_semaphore()
    for bit in here:
        pl.semaphore_signal(barrier, inc=1, device_id={"facet": here[bit]}, device_id_type=MESH)
    inner = (rank > 0, rank < pos_v - 1)
    ahead = ((rank + 1) % pos_v, (rank + pos_v - 1) % pos_v)
    upper = 2 * rank // pos_v
    for way, step in enumerate((-1, 1)):
        @pl.when(inner[way])
        def _():
            pl.semaphore_signal(
                barrier, inc=1, device_id={"sub": rank + step}, device_id_type=MESH
            )

    def corners_of(place):
        wanted = []
        for slab in range(facets):
            member = me
            for bit in bits_of(facets):
                member = flip(member, bit) if slab & bit else member
            wanted.append(member * pos_v + place)

        def note(subgrid, found):
            at = worker[subgrid]
            return tuple(jnp.where(at == w, subgrid, f) for w, f in zip(wanted, found))

        blank = tuple(jnp.int32(0) for _ in wanted)
        found = lax.fori_loop(0, worker.shape[0], note, blank, unroll=8)
        return [subgrid // pos_v for subgrid in found], [subgrid % pos_v for subgrid in found]

    tops, lefts = corners_of(rank)

    def turned(facet):
        turn = turns[facet]
        real, imag = turn[0:1], turn[1:2]
        return (base[0] * real - base[1] * imag, base[0] * imag + base[1] * real)

    def quarters(table, real, imag, flipped_first):
        table[:MC, :SUB] = real.astype(BF16)
        table[MC:, SUB:] = real.astype(BF16)
        low, high = (-imag, imag) if flipped_first else (imag, -imag)
        table[:MC, SUB:] = low.astype(BF16)
        table[MC:, :SUB] = high.astype(BF16)

    real, imag = turned(me)
    quarters(left_table, real, imag, False)
    real, imag = turned((5 * me + 3) % facets)
    b_real, b_imag = real.T, imag.T
    quarters(right_table, b_real, b_imag, True)
    for part in range(2):
        even, odd = spec[0, part], spec[0, part, :, STEP:]
        for top in range(views.shape[0]):
            at = top // 2 * 2 * STEP
            view = (odd if top % 2 else even)[:, at : at + MC]
            views[top, part] = view.reshape(cols // STEP, STEP, MC)

    @pl.when(jnp.logical_and(inner[0], inner[1]))
    def _():
        pl.semaphore_wait(barrier, 5)

    @pl.when(jnp.logical_not(jnp.logical_and(inner[0], inner[1])))
    def _():
        pl.semaphore_wait(barrier, 4)

    sent = []

    def post(source, target, sems, index, bit):
        send, recv = sems
        copy = remote(source, target, send.at[index], recv.at[index], "facet", here[bit])
        copy.start()
        sent.append(copy)

    def arrive(source, target, sems, index, bit):
        send, recv = sems
        remote(source, target, send.at[index], recv.at[index], "facet", here[bit]).wait_recv()

    def contribution(slab):
        top, left = tops[slab], lefts[slab]
        window = jnp.concatenate(
            [
                jnp.concatenate([views[top, part, left + i] for i in range(MC // STEP)], axis=0)
                for part in range(2)
            ],
            axis=1,
        )
        half = jnp.dot(window, left_table[...], preferred_element_type=F32).astype(BF16)
        half = jnp.concatenate([half[:, :SUB], half[:, SUB:]], axis=0)
        return jnp.dot(right_table[...], half, preferred_element_type=F32)

    def to_partner(slab):
        value = contribution(slab)
        out_core[slab // 2] = value.astype(BF16).reshape(2, SUB, SUB)
        post(out_core.at[slab // 2], in_core.at[slab // 2], core_sems, slab // 2, core)

    def own(slab):
        value = contribution(slab).reshape(2, SUB, SUB)
        arrive(out_core.at[slab // 2], in_core.at[slab // 2], core_sems, slab // 2, core)
        return value + in_core[slab // 2].astype(F32)

    half_rows = SUB // 2
    halves = (slice(0, half_rows), slice(half_rows, SUB))
    lanes = {axis_x: (out_x, in_x, x_sems), axis_y: (out_y, in_y, y_sems)}

    def hold(bit, part, index, value):
        lanes[bit][0][part, index] = value.astype(BF16)

    def go(bit, part, index):
        out, landing, sems = lanes[bit]
        post(out.at[part, index], landing.at[part, index], sems, (part, index), bit)

    def come(bit, part, index):
        out, landing, sems = lanes[bit]
        arrive(out.at[part, index], landing.at[part, index], sems, (part, index), bit)
        return landing[part, index].astype(F32)

    to_partner(7)
    to_partner(3)
    to_partner(5)
    value = own(6)
    for part in range(2):
        for bit, half in ((axis_x, 0), (axis_y, 1)):
            hold(bit, part, 0, value[part, halves[half]])
            if part == 0:
                go(bit, 0, 0)
    for slab, bit, near, far, keep in ((2, axis_x, 0, 1, 0), (4, axis_y, 1, 0, 1)):
        value = own(slab)
        for part in range(2):
            hold(bit, part, 1, value[part, halves[near]])
            if part == 0:
                go(bit, 0, 1)
                go(bit, 1, 0)
            kept[keep, part] = value[part, halves[far]]
    to_partner(1)
    value = own(0)
    for part in range(2):
        for half in range(2):
            kept[2 + half, part] = value[part, halves[half]]

    def turn_corner(part):
        for bit, other, keep in ((axis_x, axis_y, 0), (axis_y, axis_x, 1)):
            hold(bit, part, 2, kept[keep, part] + come(other, part, 0))
            go(bit, part, 2)

    turn_corner(0)
    go(axis_x, 1, 1)
    go(axis_y, 1, 1)

    def place(table, first, second):
        blank = jnp.zeros((SUB, cols * 2 - MC), F32)
        first = jnp.concatenate([first, blank], axis=1)
        second = pltpu.roll(jnp.concatenate([second, blank], axis=1), cols, 1)
        value = first + second
        for left in range(pos_v):
            moved = pltpu.roll(value, left * STEP, 1) if left else value
            placed_table[left, table * SUB : (table + 1) * SUB] = moved.astype(BF16)

    place(0, b_real, -b_imag)
    place(1, b_imag, b_real)
    turn_corner(1)

    def prepare(index, carry):
        span = pl.ds(pl.multiple_of(index * block, block), block)
        values, groups = compact(offsets[0, 0:1, span], fractions[0, 0:1, span])
        u_dense[:, span] = spread(values, groups.astype(jnp.int16))
        values, groups = compact(offsets[0, 1:2, span], fractions[0, 1:2, span])
        v_values[:, span] = values.astype(F32)
        v_groups[:, span] = groups
        return carry

    lax.fori_loop(0, slots // block, prepare, 0, unroll=2)

    def clear(slab, carry):
        blank = jnp.zeros((margin // CELLS, CELLS, 2 * cols), BF16)
        padded[slab, : margin // CELLS] = blank
        padded[slab, (margin + MC) // CELLS :] = blank
        return carry

    total[...] = jnp.zeros_like(total)
    live_count = count[0]

    def visit(part, index, carry):
        first = pl.multiple_of(index * block, block)
        span = pl.ds(first, block)
        u_weights = u_dense[:, span]
        values, groups = v_values[:, span], v_groups[:, span]
        product = jnp.dot(grid[part], u_weights, preferred_element_type=F32)
        bits = [(groups & bit) != 0 for bit in bits_of(SUB // CELLS)]
        live = first + lax.broadcasted_iota(jnp.int32, (1, block), 1) < live_count
        model = jnp.sum(gather_cells(product, bits) * values, axis=0, keepdims=True)
        row = jnp.where(live, observed[0, part : part + 1, span] - model, 0.0)
        residual[0, part : part + 1, span] = row
        total[part] += lax.dot_general(
            u_weights,
            spread((row * values).astype(BF16), groups.astype(jnp.int16)),
            (((1,), (1,)), ((), ())),
            preferred_element_type=F32,
        )
        return carry

    def visibilities(part):
        for bit, other, half in ((axis_x, axis_y, 0), (axis_y, axis_x, 1)):
            value = kept[2 + half, part] + come(bit, part, 1) + come(other, part, 2)
            grid[part, halves[half]] = value.astype(BF16)
        lax.fori_loop(0, slots // block, functools.partial(visit, part), 0, unroll=True)
        slabs[0, part] = total[part].astype(BF16)

    class Ring:
        def __init__(self, store, sems):
            self.store, self.sems, self.sent = store, sems, []

        def copy(self, slab, part, bit, half):
            send, recv = self.sems
            index = (slab + bit, part, half or 0)
            rows_of = slice(None) if half is None else halves[half]
            return remote(
                self.store.at[slab, part, rows_of], self.store.at[slab + bit, part, rows_of],
                send.at[index], recv.at[index], "facet", here[bit],
            )

        def share(self, slab, part, bit, half=None):
            self.copy(slab, part, bit, half).start()
            self.sent.append((slab, part, bit, half))

        def shared(self, slab, part, half=None):
            bit = slab & -slab
            self.copy(slab - bit, part, bit, half).wait_recv()

        def begin(self, part):
            for bit in (axis_x, axis_y, core):
                self.share(0, part, bit)

        def pass_on(self, part):
            for slab, bit, half in ((axis_x, axis_y, 0), (axis_y, axis_x, 1)):
                self.shared(slab, part)
                self.share(slab, part, bit, half)
                self.share(slab, part, core)

        def pass_far(self, part):
            for half in range(2):
                bit = (axis_y, axis_x)[half]
                self.copy(6 - bit, part, bit, half).wait_recv()
                self.share(6, part, core, half)

        def complete(self, slab):
            for part in range(2):
                for half in range(2) if slab == 7 else (None,):
                    self.shared(slab, part, half)

        def window(self, slab, left):
            source = self.store[slab].reshape(2 * SUB, SUB)
            half = jnp.dot(left_table[...], source, preferred_element_type=F32).astype(BF16)
            half = jnp.concatenate([half[:MC], half[MC:]], axis=1)
            window = jnp.dot(half, placed_table[left], preferred_element_type=F32)
            return window.astype(BF16).reshape(MC // CELLS, CELLS, 2 * cols)

        def settle(self):
            for item in self.sent:
                self.copy(*item).wait_send()

    ring = Ring(slabs, gather_sems)
    guests = Ring(guest_slabs, guest_sems)
    inside = slice(margin // CELLS, (margin + MC) // CELLS)

    def hand_over(way, part):
        send, recv = hand_sems
        return remote(
            slabs.at[0, part], guest_slabs.at[0, part], send.at[part], recv.at[part],
            "sub", ahead[way],
        )

    for part in range(2):
        visibilities(part)
        ring.begin(part)

        for way, spot in enumerate((0, pos_v - 1)):
            @pl.when(rank == spot)
            def _():
                hand_over(way, part).start()

    def adjoint(slab):
        padded[slab, inside] = ring.window(slab, lefts[slab])

    adjoint(0)
    ring.pass_on(0)
    ring.complete(1)
    adjoint(1)
    lax.fori_loop(0, facets, clear, 0)
    for slot in range(2):
        lone[slot, : inside.start] = jnp.zeros((inside.start, CELLS, 2 * cols), BF16)
        lone[slot, inside.stop :] = jnp.zeros((inside.start, CELLS, 2 * cols), BF16)
    extra[...] = jnp.zeros_like(extra)
    ring.pass_on(1)
    adjoint(2)
    adjoint(4)
    ring.pass_far(0)
    ring.complete(3)
    adjoint(3)
    ring.pass_far(1)

    for way, spot in enumerate((1, pos_v - 2)):
        @pl.when(rank == spot)
        def _():
            for part in range(2):
                hand_over(way, part).wait_recv()
                guests.begin(part)

    ring.complete(5)
    adjoint(5)
    adjoint(6)
    ring.complete(7)
    adjoint(7)

    piece = rows // pos_v
    spans = row_spans(piece)
    starts = [(margin - top * STEP) // CELLS for top in tops]
    guest_place = upper * (pos_v - 1)
    guest_tops, guest_lefts = corners_of(guest_place)

    def guest(slab):
        slot = slab % 2
        lone[slot, inside] = guests.window(slab, guest_lefts[slab])
        begin = (margin - guest_tops[slab] * STEP) // CELLS + rank * (piece // CELLS)
        pick = [lone[slot, begin + i] for i in range(piece // CELLS)]
        extra[...] += jnp.concatenate(pick, axis=0).astype(F32)

    def guest_tasks():
        def both(*calls):
            def run():
                for call, *args in calls:
                    call(*args)
            return run

        return [
            both((guests.pass_on, 0), (guest, 0)),
            both((guests.complete, 1), (guest, 1)),
            both((guests.pass_on, 1), (guest, 2)),
            both((guest, 4),),
            both((guests.pass_far, 0),),
            both((guests.complete, 3), (guest, 3)),
            both((guests.pass_far, 1),),
            both((guests.complete, 5), (guest, 5)),
            both((guest, 6),),
            both((guests.complete, 7), (guest, 7)),
        ]

    def own_rows(chunk, part):
        at, size = spans[part]
        value = jnp.zeros((size, 2 * cols), F32)
        for slab in range(facets):
            begin = starts[slab] + chunk * (piece // CELLS) + at // CELLS
            pick = [padded[slab, begin + i] for i in range(size // CELLS)]
            value = value + jnp.concatenate(pick, axis=0).astype(F32)
        return value

    def line_copy(way, chunk, part):
        rows_of = pl.ds(*spans[part])
        send, recv = line_sems
        return remote(
            staged.at[chunk, rows_of], landed.at[way, chunk, rows_of],
            send.at[way, chunk, part], recv.at[way, chunk, part], "sub", ahead[way],
        )

    def plan(place, mirrored):
        steps = []
        for way in range(2):
            depth = pos_v - 1 - place if way else place
            chunks = range(place) if way else range(pos_v - 1, max(place, 1), -1)
            for turn, (chunk, part) in enumerate((c, p) for c in chunks for p in range(len(spans))):
                near = pos_v - 1 - chunk if mirrored else chunk
                steps.append((turn + depth, depth, way, 1 - way if mirrored else way, near, part))
        return sorted(steps)

    for spot in range(pos_v):
        mirrored = 2 * spot >= pos_v
        place = pos_v - 1 - spot if mirrored else spot

        @pl.when(rank == spot)
        def _():
            first_sent = len(guests.sent)
            tasks = guest_tasks() if place == 1 else []
            budget, relays = len(tasks), 0
            for _, depth, away, way, chunk, part in plan(place, mirrored):
                rows_of = pl.ds(*spans[part])
                value = own_rows(chunk, part)
                if depth:
                    line_copy(way, chunk, part).wait_recv()
                    value = value + landed[way, chunk, rows_of].astype(F32)
                staged[chunk, rows_of] = value.astype(BF16)
                line_copy(way, chunk, part).start()
                if away == 0:
                    relays += 1
                    while tasks and budget - len(tasks) < relays * budget // (2 * len(spans)):
                        tasks.pop(0)()
            for task in tasks:
                task()
            for part, span in enumerate(spans):
                rows_of = pl.ds(*span)
                value = own_rows(spot, part)
                if place == 1:
                    value = value + extra[rows_of]
                for way in range(2):
                    if way != (1 if mirrored else 0) or place > 1:
                        line_copy(way, spot, part).wait_recv()
                        value = value + landed[way, spot, rows_of].astype(F32)
                update[0, 0, rows_of] = value[:, :cols]
                update[0, 1, rows_of] = value[:, cols:]
            for _, _, _, way, chunk, part in plan(place, mirrored):
                line_copy(way, chunk, part).wait_send()
            if place == 1:
                for part in range(2):
                    for bit in (axis_x, axis_y, core):
                        guests.copy(0, part, bit, None).wait_send()
                for item in guests.sent[first_sent:]:
                    guests.copy(*item).wait_send()
            if place == 0:
                for part in range(2):
                    hand_over(1 if mirrored else 0, part).wait_send()

    ring.settle()
    for copy in sent:
        copy.wait_send()


def fused(facet_spec, worker, vis_count, bin_offsets, bin_fractions, observed):
    facets = lax.axis_size("facet")
    pos_v = lax.axis_size("sub")
    rows, cols = facet_spec.shape[2:]
    slots = bin_offsets.shape[2]
    block = math.gcd(slots, 2048)
    base, turns = phases(facets)
    piece = rows // pos_v
    parts = len(row_spans(piece))
    dma = pltpu.SemaphoreType.DMA
    pair = lambda *shape: (dma(shape), dma(shape))
    return pl.pallas_call(
        functools.partial(fused_kernel, facets, pos_v, block),
        out_shape=(
            pltpu.VMEM((1, 2, slots), F32),
            pltpu.VMEM((1, 2, piece, cols), F32),
        ),
        in_specs=[VMEM, VMEM, SMEM, SMEM, VMEM, VMEM, VMEM, VMEM],
        out_specs=(VMEM, VMEM),
        scratch_shapes=[
            pltpu.VMEM((2 * MC, 2 * SUB), BF16),
            pltpu.VMEM((2 * SUB, 2 * MC), BF16),
            pltpu.VMEM((pos_v, 2 * SUB, 2 * cols), BF16),
            pltpu.VMEM(((rows - MC) // STEP + 1, 2, cols // STEP, STEP, MC), BF16),
            pltpu.VMEM((facets // 2, 2, SUB, SUB), BF16),
            pltpu.VMEM((facets // 2, 2, SUB, SUB), BF16),
            pltpu.VMEM((2, 3, SUB // 2, SUB), BF16),
            pltpu.VMEM((2, 3, SUB // 2, SUB), BF16),
            pltpu.VMEM((2, 3, SUB // 2, SUB), BF16),
            pltpu.VMEM((2, 3, SUB // 2, SUB), BF16),
            pltpu.VMEM((4, 2, SUB // 2, SUB), F32),
            pltpu.VMEM((2, SUB, SUB), BF16),
            pltpu.VMEM((SUB, slots), BF16),
            pltpu.VMEM((CELLS, slots), F32),
            pltpu.VMEM((CELLS, slots), jnp.int32),
            pltpu.VMEM((2, SUB, SUB), F32),
            pltpu.VMEM((facets, 2, SUB, SUB), BF16),
            pltpu.VMEM((facets, (2 * rows - MC) // CELLS, CELLS, 2 * cols), BF16),
            pltpu.VMEM((pos_v, piece, 2 * cols), BF16),
            pltpu.VMEM((2, pos_v, piece, 2 * cols), BF16),
            pltpu.VMEM((facets, 2, SUB, SUB), BF16),
            pltpu.VMEM((2, (2 * rows - MC) // CELLS, CELLS, 2 * cols), BF16),
            pltpu.VMEM((piece, 2 * cols), F32),
            pair(facets // 2),
            pair(2, 3),
            pair(2, 3),
            pair(facets, 2, 2),
            pair(2, pos_v, parts),
            pair(facets, 2, 2),
            pair(2),
        ],
        compiler_params=pltpu.CompilerParams(
            collective_id=3, has_side_effects=True, vmem_limit_bytes=56 * 1024 * 1024
        ),
        name="everything",
    )(
        base, turns, worker, vis_count, jnp.swapaxes(facet_spec, 2, 3),
        bin_offsets, bin_fractions, observed,
    )


def on_device(facet_spec, *rest):
    facets = lax.axis_size("facet")
    rows, cols = facet_spec.shape[2:]
    padded_bytes = facets * (2 * rows - MC) * 2 * cols * 2
    line = lax.axis_size("sub")
    fits = len(bits_of(facets)) == 3 and line >= 4 and line % 2 == 0 and padded_bytes <= 20 * 1024 * 1024
    return (fused if fits else staged_path)(facet_spec, *rest)


def solution(mesh):
    placed = (
        P("facet", None, None, None),
        P(),
        P(("facet", "sub")),
        P(("facet", "sub"), None, None),
        P(("facet", "sub"), None, None),
        P(("facet", "sub"), None, None),
    )
    return jax.shard_map(
        on_device,
        mesh=mesh,
        in_specs=placed,
        out_specs=(P(("facet", "sub"), None, None), P("facet", None, "sub", None)),
        check_vma=False,
    )
```

```python
import functools
import math

import jax
import jax.numpy as jnp
import numpy as np
from jax import lax
from jax.experimental import pallas as pl
from jax.experimental.pallas import tpu as pltpu
from jax.sharding import PartitionSpec as P

SUB = 256
MC = 256
STEP = 64
KS = 8
VB = 512
MESH = pl.DeviceIdType.MESH
VMEM = pl.BlockSpec(memory_space=pltpu.VMEM)
SMEM = pl.BlockSpec(memory_space=pltpu.SMEM)
F32 = jnp.float32
BF16 = jnp.bfloat16


def flip(index, bit):
    return index + bit - 2 * bit * ((index // bit) % 2)


def bits_of(count):
    return [1 << level for level in range(count.bit_length() - 1)]


def routes(count):
    bits = bits_of(count)
    return (bits, bits[:1] + bits[:0:-1])


def greet(count):
    me = lax.axis_index("facet")
    barrier = pltpu.get_barrier_semaphore()
    bits = bits_of(count)
    for bit in bits:
        pl.semaphore_signal(
            barrier, inc=1, device_id={"facet": flip(me, bit)}, device_id_type=MESH
        )
    pl.semaphore_wait(barrier, len(bits))


def remote(src, dst, send, recv, axis, target):
    return pltpu.make_async_remote_copy(
        src_ref=src,
        dst_ref=dst,
        send_sem=send,
        recv_sem=recv,
        device_id={axis: target},
        device_id_type=MESH,
    )


def transform_kernel(
    facets, pos_v, base, turns, worker, spec, slabs, left_adjoint, right_table,
    turned_table, corners, left_table, holder
):
    cols = spec.shape[3]
    pad = (pos_v - 1) * STEP
    me = lax.axis_index("facet")
    rank = lax.axis_index("sub")

    def note(subgrid, carry):
        holder[worker[subgrid]] = subgrid
        return carry

    lax.fori_loop(0, worker.shape[0], note, 0)
    for slab in range(facets):
        member = me
        for bit in bits_of(facets):
            member = flip(member, bit) if slab & bit else member
        subgrid = holder[member * pos_v + rank]
        corners[0, slab] = subgrid // pos_v * STEP
        corners[1, slab] = pad - subgrid % pos_v * STEP

    def turned(facet):
        turn = turns[facet]
        real, imag = turn[0:1], turn[1:2]
        return (base[0] * real - base[1] * imag, base[0] * imag + base[1] * real)

    real, imag = turned(me)
    left_adjoint[:MC, :SUB] = real.astype(BF16)
    left_adjoint[:MC, SUB:] = imag.astype(BF16)
    left_adjoint[MC:, :SUB] = (-imag).astype(BF16)
    left_adjoint[MC:, SUB:] = real.astype(BF16)
    real, imag = real.T, imag.T
    left_table[:SUB, :MC] = real.astype(BF16)
    left_table[:SUB, MC:] = (-imag).astype(BF16)
    left_table[SUB:, :MC] = imag.astype(BF16)
    left_table[SUB:, MC:] = real.astype(BF16)
    real, imag = turned((5 * me + 3) % facets)
    for table, first, second in ((right_table, real, imag), (turned_table, -imag, real)):
        table[:pad] = jnp.zeros((pad, 2 * SUB), BF16)
        table[pad + MC :] = jnp.zeros((pad, 2 * SUB), BF16)
        table[pad : pad + MC, :SUB] = first.astype(BF16)
        table[pad : pad + MC, SUB:] = second.astype(BF16)

    def transform(slab, carry):
        top = pl.multiple_of(corners[0, slab], STEP)
        left = pl.multiple_of(corners[1, slab], STEP)
        window = jnp.concatenate(
            [spec[0, 0, pl.ds(top, MC), :], spec[0, 1, pl.ds(top, MC), :]], axis=0
        )
        table = right_table[pl.ds(left, cols), :]
        mixed = jnp.dot(window, table, preferred_element_type=F32)
        real = mixed[:MC, :SUB] - mixed[MC:, SUB:]
        imag = mixed[:MC, SUB:] + mixed[MC:, :SUB]
        half = jnp.concatenate([real, imag], axis=0).astype(BF16)
        value = jnp.dot(left_table[...], half, preferred_element_type=F32)
        slabs[slab] = value.astype(BF16).reshape(2, SUB, SUB)
        return carry

    lax.fori_loop(0, facets, transform, 0, unroll=2)


def halve_kernel(facets, slabs, grid_out, total, landed, send, recv):
    me = lax.axis_index("facet")
    greet(facets)
    orders = routes(facets)
    levels = len(orders[0])
    sent = []

    def queue(part, level, held):
        rank = lambda slab: tuple(not slab & bit for bit in orders[part][level:])
        return sorted(held, key=rank)

    def copy_of(source, level, slab, part):
        bit = orders[part][level]
        return remote(
            source.at[slab, part], landed.at[level, slab - bit, part],
            send.at[2 * level + part, slab], recv.at[2 * level + part, slab - bit],
            "facet", flip(me, bit),
        )

    def post(source, level, slab, part):
        copy = copy_of(source, level, slab, part)
        copy.start()
        sent.append(copy)

    held = [list(range(facets))] * 2
    pairs = [queue(part, 0, [s for s in held[part] if s & 1]) for part in range(2)]
    for both in zip(*pairs):
        for part, slab in enumerate(both):
            post(slabs, 0, slab, part)
    for level in range(levels):
        held = [[s for s in held[p] if not s & orders[p][level]] for p in range(2)]
        pairs = [queue(part, level + 1, held[part]) for part in range(2)]
        for both in zip(*pairs):
            for part, slab in enumerate(both):
                copy_of(slabs, level, slab + orders[part][level], part).wait_recv()
                source = slabs if level == 0 else total
                value = source[slab, part].astype(F32) + landed[level, slab, part].astype(F32)
                if level == levels - 1:
                    grid_out[part] = value.astype(BF16)
                else:
                    total[slab, part] = value.astype(BF16)
                    if slab & orders[part][level + 1]:
                        post(total, level + 1, slab, part)
    for copy in sent:
        copy.wait_send()


def kernel_columns(offsets, fractions):
    cells = lax.broadcasted_iota(jnp.int32, (SUB, offsets.shape[1]), 0).astype(F32)
    scale = math.sqrt(math.log2(math.e)) * 9.0 / KS
    centred = cells - (offsets.astype(F32) + (0.5 * KS - 0.5))
    distance = centred * scale - (fractions - 0.5) * scale
    inside = jnp.abs(centred) < 0.5 * KS
    return jnp.where(inside, jnp.exp2(-1.0 - distance * distance), 0.0).astype(BF16)


def vis_kernel(count, grid, offsets, fractions, observed, residual, gridded, flipped, total):
    slots = offsets.shape[2]
    live_count = count[0]
    flipped[:SUB] = grid[0].astype(F32).T.astype(BF16)
    flipped[SUB:] = grid[1].astype(F32).T.astype(BF16)
    total[...] = jnp.zeros_like(total)
    residual[...] = jnp.zeros_like(residual)

    def half_block(first):
        span = pl.ds(first, VB)
        u_weights = kernel_columns(offsets[0, 0:1, span], fractions[0, 0:1, span])
        v_weights = kernel_columns(offsets[0, 1:2, span], fractions[0, 1:2, span])
        v_float = v_weights.astype(F32)
        product = jnp.dot(flipped[...], u_weights, preferred_element_type=F32)
        live = first + lax.broadcasted_iota(jnp.int32, (1, VB), 1) < live_count
        weighted = []
        for part in range(2):
            model = jnp.sum(product[part * SUB : (part + 1) * SUB] * v_float, axis=0, keepdims=True)
            row = jnp.where(live, observed[0, part : part + 1, span] - model, 0.0)
            residual[0, part : part + 1, span] = row
            weighted.append((row * v_float).astype(BF16))
        return lax.dot_general(
            u_weights,
            jnp.concatenate(weighted, axis=0),
            (((1,), (1,)), ((), ())),
            preferred_element_type=F32,
        )

    def block(index, carry):
        first = pl.multiple_of(index * 2 * VB, 2 * VB)
        total[...] += half_block(first) + half_block(first + VB)
        return carry

    lax.fori_loop(0, (live_count + 2 * VB - 1) // (2 * VB), block, 0)
    gridded[0] = total[:, :SUB].astype(BF16)
    gridded[1] = total[:, SUB:].astype(BF16)


def gather_kernel(facets, own, slabs, send, recv):
    me = lax.axis_index("facet")
    greet(facets)
    orders = [order[:0:-1] + order[:1] for order in routes(facets)]
    levels = len(orders[0])
    sent = []

    def copy_of(level, slab, part):
        bit = orders[part][level]
        source = slabs.at[slab, part] if slab else own.at[part]
        return remote(
            source, slabs.at[slab + bit, part],
            send.at[part, slab + bit], recv.at[part, slab + bit],
            "facet", flip(me, bit),
        )

    def post(level, slab, part):
        copy = copy_of(level, slab, part)
        copy.start()
        sent.append(copy)

    for level in range(levels):
        for part in range(2):
            post(level, 0, part)
    slabs[0] = own[...]
    held = [[0], [0]]
    for level in range(levels):
        for both in zip(*held):
            for part, slab in enumerate(both):
                copy_of(level, slab, part).wait_recv()
                for later in range(level + 1, levels):
                    post(later, slab + orders[part][level], part)
        held = [held[p] + [s + orders[p][level] for s in held[p]] for p in range(2)]
    for copy in sent:
        copy.wait_send()


def adjoint_kernel(facets, corners, everyone, left_table, right_table, turned_table, pieces, plane):
    cols = plane.shape[1] // 2
    chunk = pieces.shape[1]
    plane[...] = jnp.zeros_like(plane)

    def add_source(slab, carry):
        top = pl.multiple_of(corners[0, slab], STEP)
        left = pl.multiple_of(corners[1, slab], STEP)
        source = everyone[slab].reshape(2 * SUB, SUB)
        half = jnp.dot(left_table[...], source, preferred_element_type=F32)
        row = jnp.concatenate([half[:MC], half[MC:]], axis=1).astype(BF16)
        table = jnp.concatenate(
            [right_table[pl.ds(left, cols), :], turned_table[pl.ds(left, cols), :]], axis=0
        )
        window = lax.dot_general(row, table, (((1,), (1,)), ((), ())), preferred_element_type=F32)
        plane[pl.ds(top, MC), :] += window
        return carry

    lax.fori_loop(0, facets, add_source, 0, unroll=2)
    for piece in range(pieces.shape[0]):
        pieces[piece] = plane[piece * chunk : (piece + 1) * chunk, :].astype(BF16)


def line_kernel(groups, pieces, update, totals, landed, send, recv):
    me = lax.axis_index("sub")
    barrier = pltpu.get_barrier_semaphore()
    inner = (me > 0, me < groups - 1)
    ahead = ((me + 1) % groups, (me + groups - 1) % groups)
    behind = (ahead[1], ahead[0])
    for way in range(2):
        @pl.when(inner[way])
        def _():
            pl.semaphore_signal(
                barrier, inc=1, device_id={"sub": behind[way]}, device_id_type=MESH
            )
    between = jnp.logical_and(inner[0], inner[1])

    @pl.when(between)
    def _():
        pl.semaphore_wait(barrier, 2)

    @pl.when(jnp.logical_not(between))
    def _():
        pl.semaphore_wait(barrier, 1)

    cols = update.shape[3]
    size = pieces.shape[1]
    cut = (size // 2 + 15) // 16 * 16
    spans = (pl.ds(0, cut), pl.ds(cut, size - cut))

    def copy_of(source, way, chunk, part):
        return remote(
            source.at[chunk, spans[part]], landed.at[way, chunk, spans[part]],
            send.at[way, chunk, part], recv.at[way, chunk, part], "sub", ahead[way],
        )

    def plan(place):
        steps = []
        for way in range(2):
            depth = place if way == 0 else groups - 1 - place
            for turn in range(2 * (groups - 1 - depth)):
                chunk = turn // 2 if way else groups - 1 - turn // 2
                steps.append((turn + depth, depth, way, chunk, turn % 2))
        return sorted(steps)

    for place in range(groups):
        @pl.when(me == place)
        def _():
            for _, depth, way, chunk, part in plan(place):
                if depth == 0:
                    copy_of(pieces, way, chunk, part).start()
                    continue
                copy_of(pieces, way, chunk, part).wait_recv()
                totals[way, chunk, spans[part]] = (
                    pieces[chunk, spans[part]].astype(F32)
                    + landed[way, chunk, spans[part]].astype(F32)
                ).astype(BF16)
                copy_of(totals.at[way], way, chunk, part).start()
            for part in range(2):
                span = spans[part]
                value = pieces[place, span].astype(F32)
                for way in range(2):
                    if place != (0, groups - 1)[way]:
                        copy_of(pieces, way, place, part).wait_recv()
                        value = value + landed[way, place, span].astype(F32)
                update[0, 0, span] = value[:, :cols]
                update[0, 1, span] = value[:, cols:]
            for _, depth, way, chunk, part in plan(place):
                copy_of(pieces, way, chunk, part).wait_send()


def phases(facets):
    modulus = SUB * facets
    centred = np.arange(SUB) - SUB // 2
    base = np.exp(2j * np.pi * (np.outer(centred, centred) * facets % modulus) / modulus)
    turn = np.exp(2j * np.pi * (np.outer(np.arange(facets), centred) % modulus) / modulus)
    pair = lambda z: jnp.asarray(np.stack([z.real, z.imag]).astype(np.float32))
    return pair(base * MC ** (-0.5)), jnp.swapaxes(pair(turn), 0, 1)


def staged_path(facet_spec, worker_of_subgrid, vis_count, bin_offsets, bin_fractions, observed):
    facets = lax.axis_size("facet")
    pos_v = lax.axis_size("sub")
    rows = facet_spec.shape[2]
    cols = facet_spec.shape[3]
    pad = (pos_v - 1) * STEP
    slots = bin_offsets.shape[2]
    base, turns = phases(facets)
    levels = len(bits_of(facets))
    slab_shape = (2, SUB, SUB)
    limit = 60 * 1024 * 1024
    slabs, left_adjoint, right, right_turned, corners = pl.pallas_call(
        functools.partial(transform_kernel, facets, pos_v),
        out_shape=(
            jax.ShapeDtypeStruct((facets,) + slab_shape, BF16),
            jax.ShapeDtypeStruct((2 * MC, 2 * SUB), BF16),
            jax.ShapeDtypeStruct((MC + 2 * pad, 2 * SUB), BF16),
            jax.ShapeDtypeStruct((MC + 2 * pad, 2 * SUB), BF16),
            jax.ShapeDtypeStruct((2, facets), jnp.int32),
        ),
        in_specs=[VMEM, VMEM, SMEM, VMEM],
        out_specs=(VMEM, VMEM, VMEM, VMEM, SMEM),
        scratch_shapes=[
            pltpu.VMEM((2 * SUB, 2 * MC), BF16),
            pltpu.SMEM(worker_of_subgrid.shape, jnp.int32),
        ],
        compiler_params=pltpu.CompilerParams(vmem_limit_bytes=limit),
        name="transform",
    )(base, turns, worker_of_subgrid, facet_spec)

    grid = pl.pallas_call(
        functools.partial(halve_kernel, facets),
        out_shape=jax.ShapeDtypeStruct(slab_shape, BF16),
        in_specs=[VMEM],
        out_specs=VMEM,
        scratch_shapes=[
            pltpu.VMEM((facets,) + slab_shape, BF16),
            pltpu.VMEM((levels, facets) + slab_shape, BF16),
            pltpu.SemaphoreType.DMA((2 * levels, facets)),
            pltpu.SemaphoreType.DMA((2 * levels, facets)),
        ],
        compiler_params=pltpu.CompilerParams(
            collective_id=0, has_side_effects=True, vmem_limit_bytes=limit
        ),
        name="sum_grids",
    )(slabs)

    residual, gridded = pl.pallas_call(
        vis_kernel,
        out_shape=(
            jax.ShapeDtypeStruct((1, 2, slots), F32),
            jax.ShapeDtypeStruct(slab_shape, BF16),
        ),
        in_specs=[SMEM, VMEM, VMEM, VMEM, VMEM],
        out_specs=(VMEM, VMEM),
        scratch_shapes=[
            pltpu.VMEM((2 * SUB, SUB), BF16),
            pltpu.VMEM((SUB, 2 * SUB), F32),
        ],
        compiler_params=pltpu.CompilerParams(vmem_limit_bytes=limit),
        name="visibilities",
    )(vis_count, grid, bin_offsets, bin_fractions, observed)

    everyone = pl.pallas_call(
        functools.partial(gather_kernel, facets),
        out_shape=jax.ShapeDtypeStruct((facets,) + slab_shape, BF16),
        in_specs=[VMEM],
        out_specs=VMEM,
        scratch_shapes=[
            pltpu.SemaphoreType.DMA((2, facets)),
            pltpu.SemaphoreType.DMA((2, facets)),
        ],
        compiler_params=pltpu.CompilerParams(
            collective_id=1, has_side_effects=True, vmem_limit_bytes=limit
        ),
        name="gather_grids",
    )(gridded)

    chunk = rows // pos_v
    pieces = pl.pallas_call(
        functools.partial(adjoint_kernel, facets),
        out_shape=jax.ShapeDtypeStruct((pos_v, chunk, 2 * cols), BF16),
        in_specs=[SMEM, VMEM, VMEM, VMEM, VMEM],
        out_specs=VMEM,
        scratch_shapes=[pltpu.VMEM((rows, 2 * cols), F32)],
        compiler_params=pltpu.CompilerParams(vmem_limit_bytes=limit),
        name="adjoint",
    )(corners, everyone, left_adjoint, right, right_turned)

    update = pl.pallas_call(
        functools.partial(line_kernel, pos_v),
        out_shape=jax.ShapeDtypeStruct((1, 2, chunk, cols), F32),
        in_specs=[VMEM],
        out_specs=VMEM,
        scratch_shapes=[
            pltpu.VMEM((2, pos_v, chunk, 2 * cols), BF16),
            pltpu.VMEM((2, pos_v, chunk, 2 * cols), BF16),
            pltpu.SemaphoreType.DMA((2, pos_v, 2)),
            pltpu.SemaphoreType.DMA((2, pos_v, 2)),
        ],
        compiler_params=pltpu.CompilerParams(
            collective_id=2, has_side_effects=True, vmem_limit_bytes=limit
        ),
        name="sum_pieces",
    )(pieces)
    return (residual, update)


CELLS = 16
FILL = 3


def spread(values, groups):
    zero = jnp.zeros_like(values)
    rows = [jnp.where(groups == cell, values, zero) for cell in range(SUB // CELLS)]
    return jnp.concatenate(rows, axis=0)


def compact(offsets, fractions):
    row = lax.broadcasted_iota(jnp.int32, (CELLS, offsets.shape[1]), 0)
    ahead = (row - offsets) & (CELLS - 1)
    scale = math.sqrt(math.log2(math.e)) * 9.0 / KS
    distance = (ahead.astype(F32) - (0.5 * KS - 1.0) - fractions) * scale
    values = jnp.where(ahead < KS, jnp.exp2(-1.0 - distance * distance), 0.0)
    return values.astype(BF16), (offsets + ahead) // CELLS


def gather_cells(product, bits):
    parts = [product[i * CELLS : (i + 1) * CELLS] for i in range(SUB // CELLS)]
    for bit in bits:
        parts = [jnp.where(bit, b, a) for a, b in zip(parts[::2], parts[1::2])]
    return parts[0]


def row_spans(size):
    step = (size // FILL + 15) // 16 * 16
    return [(at, min(step, size - at)) for at in range(0, size, step)]


def fused_kernel(
    facets, pos_v, block, base, turns, worker, count, spec, offsets, fractions, observed,
    residual, update, left_table, right_table, placed_table, views, out_core, in_core,
    out_x, out_y, in_x, in_y, kept, grid, u_dense, v_values, v_groups, total, slabs, padded,
    staged, landed, guest_slabs, lone, extra, mine, core_sems, x_sems, y_sems, gather_sems,
    line_sems, guest_sems, hand_sems
):
    me = lax.axis_index("facet")
    rank = lax.axis_index("sub")
    cols, rows = spec.shape[2], spec.shape[3]
    slots = offsets.shape[2]
    margin = rows - MC
    core, axis_x, axis_y = 1, 2, 4
    here = {bit: flip(me, bit) for bit in (core, axis_x, axis_y)}

    barrier = pltpu.get_barrier_semaphore()
    for bit in here:
        pl.semaphore_signal(barrier, inc=1, device_id={"facet": here[bit]}, device_id_type=MESH)
    inner = (rank > 0, rank < pos_v - 1)
    ahead = ((rank + 1) % pos_v, (rank + pos_v - 1) % pos_v)
    upper = 2 * rank // pos_v
    for way, step in enumerate((-1, 1)):
        @pl.when(inner[way])
        def _():
            pl.semaphore_signal(
                barrier, inc=1, device_id={"sub": rank + step}, device_id_type=MESH
            )

    def corners_of(place):
        wanted = []
        for slab in range(facets):
            member = me
            for bit in bits_of(facets):
                member = flip(member, bit) if slab & bit else member
            wanted.append(member * pos_v + place)

        def note(subgrid, found):
            at = worker[subgrid]
            return tuple(jnp.where(at == w, subgrid, f) for w, f in zip(wanted, found))

        blank = tuple(jnp.int32(0) for _ in wanted)
        found = lax.fori_loop(0, worker.shape[0], note, blank, unroll=8)
        return [subgrid // pos_v for subgrid in found], [subgrid % pos_v for subgrid in found]

    tops, lefts = corners_of(rank)

    def turned(facet):
        turn = turns[facet]
        real, imag = turn[0:1], turn[1:2]
        return (base[0] * real - base[1] * imag, base[0] * imag + base[1] * real)

    def quarters(table, real, imag, flipped_first):
        table[:MC, :SUB] = real.astype(BF16)
        table[MC:, SUB:] = real.astype(BF16)
        low, high = (-imag, imag) if flipped_first else (imag, -imag)
        table[:MC, SUB:] = low.astype(BF16)
        table[MC:, :SUB] = high.astype(BF16)

    real, imag = turned(me)
    quarters(left_table, real, imag, False)
    real, imag = turned((5 * me + 3) % facets)
    b_real, b_imag = real.T, imag.T
    quarters(right_table, b_real, b_imag, True)
    for part in range(2):
        even, odd = spec[0, part], spec[0, part, :, STEP:]
        for top in range(views.shape[0]):
            at = top // 2 * 2 * STEP
            view = (odd if top % 2 else even)[:, at : at + MC]
            views[top, part] = view.reshape(cols // STEP, STEP, MC)

    @pl.when(jnp.logical_and(inner[0], inner[1]))
    def _():
        pl.semaphore_wait(barrier, 5)

    @pl.when(jnp.logical_not(jnp.logical_and(inner[0], inner[1])))
    def _():
        pl.semaphore_wait(barrier, 4)

    sent = []

    def post(source, target, sems, index, bit):
        send, recv = sems
        copy = remote(source, target, send.at[index], recv.at[index], "facet", here[bit])
        copy.start()
        sent.append(copy)

    def arrive(source, target, sems, index, bit):
        send, recv = sems
        remote(source, target, send.at[index], recv.at[index], "facet", here[bit]).wait_recv()

    def contribution(slab):
        top, left = tops[slab], lefts[slab]
        window = jnp.concatenate(
            [
                jnp.concatenate([views[top, part, left + i] for i in range(MC // STEP)], axis=0)
                for part in range(2)
            ],
            axis=1,
        )
        half = jnp.dot(window, left_table[...], preferred_element_type=F32).astype(BF16)
        half = jnp.concatenate([half[:, :SUB], half[:, SUB:]], axis=0)
        return jnp.dot(right_table[...], half, preferred_element_type=F32)

    def to_partner(slab):
        value = contribution(slab)
        out_core[slab // 2] = value.astype(BF16).reshape(2, SUB, SUB)
        post(out_core.at[slab // 2], in_core.at[slab // 2], core_sems, slab // 2, core)

    def own(slab):
        value = contribution(slab).reshape(2, SUB, SUB)
        arrive(out_core.at[slab // 2], in_core.at[slab // 2], core_sems, slab // 2, core)
        return value + in_core[slab // 2].astype(F32)

    half_rows = SUB // 2
    halves = (slice(0, half_rows), slice(half_rows, SUB))
    lanes = {axis_x: (out_x, in_x, x_sems), axis_y: (out_y, in_y, y_sems)}

    def hold(bit, part, index, value):
        lanes[bit][0][part, index] = value.astype(BF16)

    def go(bit, part, index):
        out, landing, sems = lanes[bit]
        post(out.at[part, index], landing.at[part, index], sems, (part, index), bit)

    def come(bit, part, index):
        out, landing, sems = lanes[bit]
        arrive(out.at[part, index], landing.at[part, index], sems, (part, index), bit)
        return landing[part, index].astype(F32)

    to_partner(7)
    to_partner(3)
    to_partner(5)
    value = own(6)
    for part in range(2):
        for bit, half in ((axis_x, 0), (axis_y, 1)):
            hold(bit, part, 0, value[part, halves[half]])
            if part == 0:
                go(bit, 0, 0)
    for slab, bit, near, far, keep in ((2, axis_x, 0, 1, 0), (4, axis_y, 1, 0, 1)):
        value = own(slab)
        for part in range(2):
            hold(bit, part, 1, value[part, halves[near]])
            if part == 0:
                go(bit, 0, 1)
                go(bit, 1, 0)
            kept[keep, part] = value[part, halves[far]]
    to_partner(1)
    value = own(0)
    for part in range(2):
        for half in range(2):
            kept[2 + half, part] = value[part, halves[half]]

    def turn_corner(part):
        for bit, other, keep in ((axis_x, axis_y, 0), (axis_y, axis_x, 1)):
            hold(bit, part, 2, kept[keep, part] + come(other, part, 0))
            go(bit, part, 2)

    turn_corner(0)
    go(axis_x, 1, 1)
    go(axis_y, 1, 1)

    def place(table, first, second):
        blank = jnp.zeros((SUB, cols * 2 - MC), F32)
        first = jnp.concatenate([first, blank], axis=1)
        second = pltpu.roll(jnp.concatenate([second, blank], axis=1), cols, 1)
        value = first + second
        for left in range(pos_v):
            moved = pltpu.roll(value, left * STEP, 1) if left else value
            placed_table[left, table * SUB : (table + 1) * SUB] = moved.astype(BF16)

    place(0, b_real, -b_imag)
    place(1, b_imag, b_real)
    turn_corner(1)

    def prepare(index, carry):
        span = pl.ds(pl.multiple_of(index * block, block), block)
        values, groups = compact(offsets[0, 0:1, span], fractions[0, 0:1, span])
        u_dense[:, span] = spread(values, groups.astype(jnp.int16))
        values, groups = compact(offsets[0, 1:2, span], fractions[0, 1:2, span])
        v_values[:, span] = values.astype(F32)
        v_groups[:, span] = groups
        return carry

    lax.fori_loop(0, slots // block, prepare, 0, unroll=2)

    def clear(slab, carry):
        blank = jnp.zeros((margin // CELLS, CELLS, 2 * cols), BF16)
        padded[slab, : margin // CELLS] = blank
        padded[slab, (margin + MC) // CELLS :] = blank
        return carry

    total[...] = jnp.zeros_like(total)
    live_count = count[0]

    def visit(part, index, carry):
        first = pl.multiple_of(index * block, block)
        span = pl.ds(first, block)
        u_weights = u_dense[:, span]
        values, groups = v_values[:, span], v_groups[:, span]
        product = jnp.dot(grid[part], u_weights, preferred_element_type=F32)
        bits = [(groups & bit) != 0 for bit in bits_of(SUB // CELLS)]
        live = first + lax.broadcasted_iota(jnp.int32, (1, block), 1) < live_count
        model = jnp.sum(gather_cells(product, bits) * values, axis=0, keepdims=True)
        row = jnp.where(live, observed[0, part : part + 1, span] - model, 0.0)
        residual[0, part : part + 1, span] = row
        total[part] += lax.dot_general(
            u_weights,
            spread((row * values).astype(BF16), groups.astype(jnp.int16)),
            (((1,), (1,)), ((), ())),
            preferred_element_type=F32,
        )
        return carry

    def visibilities(part):
        for bit, other, half in ((axis_x, axis_y, 0), (axis_y, axis_x, 1)):
            value = kept[2 + half, part] + come(bit, part, 1) + come(other, part, 2)
            grid[part, halves[half]] = value.astype(BF16)
        lax.fori_loop(0, slots // block, functools.partial(visit, part), 0, unroll=True)
        slabs[0, part] = total[part].astype(BF16)

    class Ring:
        def __init__(self, store, sems):
            self.store, self.sems, self.sent = store, sems, []

        def copy(self, slab, part, bit, half):
            send, recv = self.sems
            index = (slab + bit, part, half or 0)
            rows_of = slice(None) if half is None else halves[half]
            return remote(
                self.store.at[slab, part, rows_of], self.store.at[slab + bit, part, rows_of],
                send.at[index], recv.at[index], "facet", here[bit],
            )

        def share(self, slab, part, bit, half=None):
            self.copy(slab, part, bit, half).start()
            self.sent.append((slab, part, bit, half))

        def shared(self, slab, part, half=None):
            bit = slab & -slab
            self.copy(slab - bit, part, bit, half).wait_recv()

        def begin(self, part):
            for bit in (axis_x, axis_y, core):
                self.share(0, part, bit)

        def pass_on(self, part):
            for slab, bit, half in ((axis_x, axis_y, 0), (axis_y, axis_x, 1)):
                self.shared(slab, part)
                self.share(slab, part, bit, half)
                self.share(slab, part, core)

        def pass_far(self, part):
            for half in range(2):
                bit = (axis_y, axis_x)[half]
                self.copy(6 - bit, part, bit, half).wait_recv()
                self.share(6, part, core, half)

        def complete(self, slab):
            for part in range(2):
                for half in range(2) if slab == 7 else (None,):
                    self.shared(slab, part, half)

        def window(self, slab, left):
            source = self.store[slab].reshape(2 * SUB, SUB)
            half = jnp.dot(left_table[...], source, preferred_element_type=F32).astype(BF16)
            half = jnp.concatenate([half[:MC], half[MC:]], axis=1)
            window = jnp.dot(half, placed_table[left], preferred_element_type=F32)
            return window.astype(BF16).reshape(MC // CELLS, CELLS, 2 * cols)

        def settle(self):
            for item in self.sent:
                self.copy(*item).wait_send()

    ring = Ring(slabs, gather_sems)
    guests = Ring(guest_slabs, guest_sems)
    inside = slice(margin // CELLS, (margin + MC) // CELLS)

    def hand_over(way, part):
        send, recv = hand_sems
        return remote(
            slabs.at[0, part], guest_slabs.at[0, part], send.at[part], recv.at[part],
            "sub", ahead[way],
        )

    for part in range(2):
        visibilities(part)
        ring.begin(part)

        for way, spot in enumerate((0, pos_v - 1)):
            @pl.when(rank == spot)
            def _():
                hand_over(way, part).start()

    def adjoint(slab):
        padded[slab, inside] = ring.window(slab, lefts[slab])

    adjoint(0)
    ring.pass_on(0)
    ring.complete(1)
    adjoint(1)
    lax.fori_loop(0, facets, clear, 0)
    for slot in range(2):
        lone[slot, : inside.start] = jnp.zeros((inside.start, CELLS, 2 * cols), BF16)
        lone[slot, inside.stop :] = jnp.zeros((inside.start, CELLS, 2 * cols), BF16)
    extra[...] = jnp.zeros_like(extra)
    ring.pass_on(1)
    adjoint(2)
    adjoint(4)
    ring.pass_far(0)
    ring.complete(3)
    adjoint(3)
    ring.pass_far(1)

    for way, spot in enumerate((1, pos_v - 2)):
        @pl.when(rank == spot)
        def _():
            for part in range(2):
                hand_over(way, part).wait_recv()
                guests.begin(part)

    ring.complete(5)
    adjoint(5)
    adjoint(6)
    ring.complete(7)
    adjoint(7)

    piece = rows // pos_v
    spans = row_spans(piece)
    starts = [(margin - top * STEP) // CELLS for top in tops]
    guest_place = upper * (pos_v - 1)
    guest_tops, guest_lefts = corners_of(guest_place)

    def guest(slab):
        slot = slab % 2
        lone[slot, inside] = guests.window(slab, guest_lefts[slab])
        begin = (margin - guest_tops[slab] * STEP) // CELLS + rank * (piece // CELLS)
        pick = [lone[slot, begin + i] for i in range(piece // CELLS)]
        extra[...] += jnp.concatenate(pick, axis=0).astype(F32)

    def guest_tasks():
        def both(*calls):
            def run():
                for call, *args in calls:
                    call(*args)
            return run

        return [
            both((guests.pass_on, 0), (guest, 0)),
            both((guests.complete, 1), (guest, 1)),
            both((guests.pass_on, 1), (guest, 2)),
            both((guest, 4),),
            both((guests.pass_far, 0),),
            both((guests.complete, 3), (guest, 3)),
            both((guests.pass_far, 1),),
            both((guests.complete, 5), (guest, 5)),
            both((guest, 6),),
            both((guests.complete, 7), (guest, 7)),
        ]

    def own_rows(chunk, part):
        at, size = spans[part]

        def tile(index, carry):
            value = jnp.zeros((CELLS, 2 * cols), F32)
            for slab in range(facets):
                begin = starts[slab] + chunk * (piece // CELLS) + at // CELLS
                value = value + padded[slab, begin + index].astype(F32)
            mine[index] = value
            return carry

        lax.fori_loop(0, size // CELLS, tile, 0)
        return mine[: size // CELLS].reshape(size, 2 * cols)

    def line_copy(way, chunk, part):
        rows_of = pl.ds(*spans[part])
        send, recv = line_sems
        return remote(
            staged.at[chunk, rows_of], landed.at[way, chunk, rows_of],
            send.at[way, chunk, part], recv.at[way, chunk, part], "sub", ahead[way],
        )

    def plan(place, mirrored):
        steps = []
        for way in range(2):
            depth = pos_v - 1 - place if way else place
            chunks = range(place) if way else range(pos_v - 1, max(place, 1), -1)
            for turn, (chunk, part) in enumerate((c, p) for c in chunks for p in range(len(spans))):
                near = pos_v - 1 - chunk if mirrored else chunk
                steps.append((turn + depth, depth, way, 1 - way if mirrored else way, near, part))
        return sorted(steps)

    def relay(depth, way, chunk, part):
        rows_of = pl.ds(*spans[part])
        value = own_rows(chunk, part)
        if depth:
            line_copy(way, chunk, part).wait_recv()
            value = value + landed[way, chunk, rows_of].astype(F32)
        staged[chunk, rows_of] = value.astype(BF16)
        line_copy(way, chunk, part).start()

    sides = [2 * spot >= pos_v for spot in range(pos_v)]
    places = [pos_v - 1 - spot if side else spot for spot, side in enumerate(sides)]
    plans = [plan(place, side) for place, side in zip(places, sides)]
    hosts = jnp.logical_or(rank == 1, rank == pos_v - 2)
    first_sent = len(guests.sent)
    tasks = guest_tasks()
    budget, relays = len(tasks), 0
    for step in range(max(len(steps) for steps in plans)):
        for spot in range(pos_v):
            if step < len(plans[spot]):
                @pl.when(rank == spot)
                def _():
                    _, depth, _, *rest = plans[spot][step]
                    relay(depth, *rest)
        if step < len(plans[1]) and plans[1][step][2] == 0:
            relays += 1
            due = relays * budget // (2 * len(spans)) - (budget - len(tasks))

            @pl.when(hosts)
            def _():
                for task in tasks[:due]:
                    task()

            tasks = tasks[due:]

    for spot in range(pos_v):
        mirrored, place = sides[spot], places[spot]

        @pl.when(rank == spot)
        def _():
            for part, span in enumerate(spans):
                rows_of = pl.ds(*span)
                value = own_rows(spot, part)
                if place == 1:
                    value = value + extra[rows_of]
                for way in range(2):
                    if way != (1 if mirrored else 0) or place > 1:
                        line_copy(way, spot, part).wait_recv()
                        value = value + landed[way, spot, rows_of].astype(F32)
                update[0, 0, rows_of] = value[:, :cols]
                update[0, 1, rows_of] = value[:, cols:]
            for _, _, _, way, chunk, part in plans[spot]:
                line_copy(way, chunk, part).wait_send()
            if place == 0:
                for part in range(2):
                    hand_over(1 if mirrored else 0, part).wait_send()

    @pl.when(hosts)
    def _():
        for part in range(2):
            for bit in (axis_x, axis_y, core):
                guests.copy(0, part, bit, None).wait_send()
        for item in guests.sent[first_sent:]:
            guests.copy(*item).wait_send()

    ring.settle()
    for copy in sent:
        copy.wait_send()


def fused(facet_spec, worker, vis_count, bin_offsets, bin_fractions, observed):
    facets = lax.axis_size("facet")
    pos_v = lax.axis_size("sub")
    rows, cols = facet_spec.shape[2:]
    slots = bin_offsets.shape[2]
    block = math.gcd(slots, 2048)
    base, turns = phases(facets)
    piece = rows // pos_v
    parts = len(row_spans(piece))
    dma = pltpu.SemaphoreType.DMA
    pair = lambda *shape: (dma(shape), dma(shape))
    return pl.pallas_call(
        functools.partial(fused_kernel, facets, pos_v, block),
        out_shape=(
            pltpu.VMEM((1, 2, slots), F32),
            pltpu.VMEM((1, 2, piece, cols), F32),
        ),
        in_specs=[VMEM, VMEM, SMEM, SMEM, VMEM, VMEM, VMEM, VMEM],
        out_specs=(VMEM, VMEM),
        scratch_shapes=[
            pltpu.VMEM((2 * MC, 2 * SUB), BF16),
            pltpu.VMEM((2 * SUB, 2 * MC), BF16),
            pltpu.VMEM((pos_v, 2 * SUB, 2 * cols), BF16),
            pltpu.VMEM(((rows - MC) // STEP + 1, 2, cols // STEP, STEP, MC), BF16),
            pltpu.VMEM((facets // 2, 2, SUB, SUB), BF16),
            pltpu.VMEM((facets // 2, 2, SUB, SUB), BF16),
            pltpu.VMEM((2, 3, SUB // 2, SUB), BF16),
            pltpu.VMEM((2, 3, SUB // 2, SUB), BF16),
            pltpu.VMEM((2, 3, SUB // 2, SUB), BF16),
            pltpu.VMEM((2, 3, SUB // 2, SUB), BF16),
            pltpu.VMEM((4, 2, SUB // 2, SUB), F32),
            pltpu.VMEM((2, SUB, SUB), BF16),
            pltpu.VMEM((SUB, slots), BF16),
            pltpu.VMEM((CELLS, slots), F32),
            pltpu.VMEM((CELLS, slots), jnp.int32),
            pltpu.VMEM((2, SUB, SUB), F32),
            pltpu.VMEM((facets, 2, SUB, SUB), BF16),
            pltpu.VMEM((facets, (2 * rows - MC) // CELLS, CELLS, 2 * cols), BF16),
            pltpu.VMEM((pos_v, piece, 2 * cols), BF16),
            pltpu.VMEM((2, pos_v, piece, 2 * cols), BF16),
            pltpu.VMEM((facets, 2, SUB, SUB), BF16),
            pltpu.VMEM((2, (2 * rows - MC) // CELLS, CELLS, 2 * cols), BF16),
            pltpu.VMEM((piece, 2 * cols), F32),
            pltpu.VMEM((piece // CELLS, CELLS, 2 * cols), F32),
            pair(facets // 2),
            pair(2, 3),
            pair(2, 3),
            pair(facets, 2, 2),
            pair(2, pos_v, parts),
            pair(facets, 2, 2),
            pair(2),
        ],
        compiler_params=pltpu.CompilerParams(
            collective_id=3, has_side_effects=True, vmem_limit_bytes=56 * 1024 * 1024
        ),
        name="everything",
    )(
        base, turns, worker, vis_count, jnp.swapaxes(facet_spec, 2, 3),
        bin_offsets, bin_fractions, observed,
    )


def on_device(facet_spec, *rest):
    facets = lax.axis_size("facet")
    rows, cols = facet_spec.shape[2:]
    padded_bytes = facets * (2 * rows - MC) * 2 * cols * 2
    line = lax.axis_size("sub")
    fits = len(bits_of(facets)) == 3 and line >= 4 and line % 2 == 0 and padded_bytes <= 20 * 1024 * 1024
    return (fused if fits else staged_path)(facet_spec, *rest)


def solution(mesh):
    placed = (
        P("facet", None, None, None),
        P(),
        P(("facet", "sub")),
        P(("facet", "sub"), None, None),
        P(("facet", "sub"), None, None),
        P(("facet", "sub"), None, None),
    )
    return jax.shard_map(
        on_device,
        mesh=mesh,
        in_specs=placed,
        out_specs=(P(("facet", "sub"), None, None), P("facet", None, "sub", None)),
        check_vma=False,
    )
```
